512 devices in a mesh: league: 128 (over z, x_hi, y), rep: 4 (over x_lo, core).
Axes of the slice: x: 4 (x_hi: 2, x_lo: 2; x = x_hi * 2 + x_lo), y: 8, z: 8, core: 2. Of those that a mesh axis runs over, the one named last changes fastest.
Arguments:
- observations: bfloat16 [65536, 2048], P(('league', 'rep')), may hold values from -6 to 6
- weights: bfloat16 [128, 2048, 2048], P('league', None, 'rep'), may hold values from -0.125 to 0.125
- gains: float32 [128, 2048], P('league'), may hold values from 0.5 to 1.5
- heads: bfloat16 [128, 2048], P('league', 'rep'), may hold values from -0.125 to 0.125
- pairing: int32 [65536, 1], P(('league', 'rep')), may hold values from 0 to 127; in each aligned block of 128 rows (0 to 127, 128 to 255, ...) at most 2 rows name the same one
- valid: int32 [65536], P(('league', 'rep')), may hold values 0 or 1
Outputs:
- own_value: float32 [65536], P(('league', 'rep'))
- opponent_value: float32 [65536], P(('league', 'rep'))
The draws below stay inside these ranges and needn't reach their ends.
Inputs may be any that keep to these rules, and one draw needn't show every extreme that they name: `pairing`: among the rows of one device, at most 2 name one agent; every agent is named by some row of the whole batch.
All inputs are finite; a program needn't handle non-finite values. No bound on the sum of `valid` on one device may be relied on, other than what follows from the above.
Results may differ from the reference program's by a relative error of at most 0.003.
Values may be sent and summed in bfloat16 or wider, within the bound.
No kernel may reach another device: no remote copies, remote signals or barrier semaphores. Data moves between devices by JAX's collectives and lax.ppermute only.
A program may use at most 64 MiB of HBM per device.

```python
import math
import jax
import jax.numpy as jnp
import numpy as np
from jax import lax

D = 2048
R_DEV = 128
AGENTS = 128
CAP = 2
ROWS = 65536
N_LEAGUE = 128
N_REP = 4


def place_ends(values, own_key, smallest, largest):
    spot = [jax.random.randint(jax.random.fold_in(own_key, axis), (), 0, length) for axis, length in enumerate(values.shape)]
    main_axis = values.shape.index(max(values.shape))
    neighbour = spot[:main_axis] + [(spot[main_axis] + 1) % values.shape[main_axis]] + spot[main_axis + 1:]
    return values.at[tuple(spot)].set(smallest).at[tuple(neighbour)].set(largest)


def levels(rng, extent, shards, low, high):
    def one(position, blocks):
        heights = jax.random.uniform(jax.random.fold_in(jax.random.fold_in(rng, 6), position), (blocks,), jnp.float32, low / len(shards), high / len(shards))
        return jnp.repeat(jnp.exp(heights), extent[position] // blocks).reshape((-1,) + (1,) * (len(extent) - position - 1))

    gain = one(*shards[0])
    for cut in shards[1:]:
        gain = gain * one(*cut)
    return gain


def shared_out(stream_key, own, number, rows, amount, top, most, skew):
    sequence = jax.random.permutation(stream_key, amount)
    crowded, usual = load_shares(amount, rows * top, most, skew, True), load_shares(amount, rows * top, most, skew, False)
    places = jnp.arange(amount)

    def named(tallies, rotation):
        used = int((tallies > 0).sum())
        fixed = max(1, used // 4)
        shifted = fixed + (places - fixed + rotation * (used - fixed)) % max(1, amount - fixed)
        return jnp.zeros((amount,), jnp.int32).at[sequence[jnp.where(places < fixed, places, shifted)]].set(jnp.asarray(tallies, jnp.int32))

    tallies = jnp.where(number % 4 == 0, named(crowded, number // 4), named(usual, number - number // 4 - 1))
    mixed = jax.random.permutation(jax.random.fold_in(own, 3), amount)
    donor, receiver = mixed[0:amount // 2 * 2:2], mixed[1:amount // 2 * 2:2]
    margin = jnp.minimum(tallies[donor] - 1, most - tallies[receiver]) // 2
    margin = jnp.where((donor == sequence[0]) | (receiver == sequence[0]) | (tallies[receiver] == 0), 0, jnp.maximum(margin, 0))
    shifted = jax.random.randint(jax.random.fold_in(own, 4), (amount // 2,), 0, 1 << 20) % (margin + 1)
    tallies = tallies.at[donor].add(-shifted).at[receiver].add(shifted)
    labels = jnp.searchsorted(jnp.cumsum(tallies), jnp.arange(rows * top), side="right").astype(jnp.int32)
    grid = labels.reshape(top, rows).T
    grid = grid[jax.random.permutation(jax.random.fold_in(own, 1), rows)]
    rotation = jax.random.randint(jax.random.fold_in(own, 2), (rows, 1), 0, top)
    return jnp.take_along_axis(grid, (jnp.arange(top)[None, :] + rotation) % top, axis=1)


def load_shares(amount, total, most, slope, full):
    loads = [(1 << 20) // math.isqrt(standing ** slope) + 1 for standing in range(1, amount + 1)]
    largest = most if full else min(most, max(-(-total // amount), total * loads[0] // sum(loads)))
    least = 1 if total - largest >= amount - 1 else 0
    counts, rest = [largest] + [least] * (amount - 1), total - largest - least * (amount - 1)
    while rest > 0:
        free = [i for i in range(1, amount) if counts[i] < largest] or [i for i in range(1, amount) if counts[i] < most]
        whole, left = sum([loads[i] for i in free]), rest
        for i in free:
            more = min(most - counts[i], max(1, left * loads[i] // whole), rest)
            counts[i] = counts[i] + more
            rest = rest - more
    return np.array(counts)


def bell_draw(key, extent, deviation, reach, shards=(), kind=jnp.bfloat16):
    drawn = jax.random.normal(key, extent, jnp.float32) * deviation
    if len(shards) > 0:
        drawn = levels(key, extent, shards, -0.22, 0.18) * drawn
    return jnp.clip(drawn, min=-reach, max=reach).astype(kind)


def setup_inputs(seed: int = 0) -> dict:
    streams_of = jax.random.split(jax.random.key(seed), 7)
    observations = bell_draw(streams_of[0], (ROWS, D), 1.0, 6.0, ((0, 512),))
    weights = bell_draw(streams_of[1], (AGENTS, D, D), D ** -0.5, 0.125, ((0, 128), (2, 4)))
    gains = jnp.clip(1.0 + 0.1 * jax.random.normal(streams_of[2], (AGENTS, D), jnp.float32), 0.5, 1.5)
    heads = bell_draw(streams_of[3], (AGENTS, D), D ** -0.5, 0.125, ((0, 128), (1, 4)))
    pairing_keys = jax.random.split(jax.random.fold_in(streams_of[4], 1), ROWS // R_DEV)
    pairing_turns = jax.random.permutation(jax.random.fold_in(streams_of[4], 3), ROWS // R_DEV)
    pairing = jax.vmap(lambda own, number: shared_out(jax.random.fold_in(streams_of[4], 2), own, number, R_DEV, AGENTS, 1, CAP, 2))(pairing_keys, pairing_turns).reshape((ROWS, 1))
    valid = place_ends((jax.random.randint(streams_of[5], (ROWS,), 0, 4) < 3).astype(jnp.int32), jax.random.fold_in(streams_of[5], 1), 0, 1)
    return dict(observations=observations, weights=weights, gains=gains, heads=heads, pairing=pairing, valid=valid)


def normed_values(obs_rows, agent_gain, weight_cols, head_cols):
    wide_rows = obs_rows.astype(jnp.float32)
    squares = lax.optimization_barrier(jnp.mean(wide_rows * wide_rows, axis=1, keepdims=True))
    scaled = (wide_rows * lax.rsqrt(squares + 1e-06) * agent_gain).astype(jnp.bfloat16)
    hidden = jax.nn.silu(jnp.dot(scaled, weight_cols, preferred_element_type=jnp.float32))
    return lax.optimization_barrier(jnp.sum(hidden * head_cols.astype(jnp.float32), axis=1))

def own_block(inputs):
    block_rows, agent_gain, weight_full, head_full = inputs
    return normed_values(block_rows, agent_gain, weight_full, head_full)

def reference(observations, weights, gains, heads, pairing, valid):
    total_rows, feature_width = observations.shape
    per_agent = total_rows // AGENTS
    blocks = observations.reshape(AGENTS, per_agent, feature_width)
    own_value = lax.map(own_block, (blocks, gains, weights, heads)).reshape(total_rows)
    owner_id = pairing[:, 0].astype(jnp.int32)
    row_order = jnp.argsort(owner_id, stable=True).astype(jnp.int32)
    most_rows = N_LEAGUE * N_REP * CAP
    padded_order = jnp.concatenate([row_order, jnp.full((most_rows,), total_rows, jnp.int32)])
    padded_obs = jnp.concatenate([observations, jnp.zeros((1, feature_width), observations.dtype)])
    slot_iota = jnp.arange(most_rows, dtype=jnp.int32)

    def visit(collected, inputs):
        agent_id, agent_gain, weight_full, head_full = inputs
        first_row = jnp.sum((owner_id < agent_id).astype(jnp.int32)).astype(jnp.int32)
        row_count = jnp.sum((owner_id == agent_id).astype(jnp.int32)).astype(jnp.int32)
        row_index = lax.dynamic_slice_in_dim(padded_order, first_row, most_rows)
        row_values = normed_values(padded_obs[row_index], agent_gain, weight_full, head_full)
        target = jnp.where(slot_iota < row_count, row_index, total_rows)
        return (collected.at[target].set(row_values), None)
    agent_ids = jnp.arange(AGENTS, dtype=jnp.int32)
    collected, unused = lax.scan(visit, jnp.zeros((total_rows + 1,), jnp.float32), (agent_ids, gains, weights, heads))
    opponent_value = jnp.where(valid == 1, collected[:total_rows], jnp.zeros((total_rows,), jnp.float32))
    return (own_value, opponent_value)
```

```python
import jax
import jax.numpy as jnp
from jax import lax
from jax.sharding import Mesh, PartitionSpec as P

NZ, NXH, NY, NXL, NC = 8, 2, 8, 2, 2
AXES = ("z", "xh", "y", "xl", "c")
SWAP = [(0, 1), (1, 0)]
CHUNKS = (256, 128, 128)


def exchange_groups():
    groups = []
    for flip in range(2):
        group = []
        for z in range(NZ):
            for xh in range(NXH):
                for y in range(NY):
                    group.append(((z * NXH + xh) * NY + y) * NXL + (xh ^ flip))
        groups.append(group)
    return groups


def scaled_rows(rows, gain):
    wide = rows.astype(jnp.float32)
    squares = jnp.mean(wide * wide, axis=1, keepdims=True)
    return (wide * lax.rsqrt(squares + 1e-06) * gain).astype(jnp.bfloat16)


def partial_values(scaled, weight, head):
    hidden = jax.nn.silu(jnp.dot(scaled, weight, preferred_element_type=jnp.float32))
    return jnp.sum(hidden * head.astype(jnp.float32), axis=1)


def per_device(observations, weights, gains, heads, pairing, valid):
    rows_dev, width = observations.shape
    n_agents = NZ * NXH * NY
    groups = exchange_groups()
    gain = gains[0]
    own_w = weights[0]
    exchange = ("z", "xh", "y", "xl")

    sib_w = lax.ppermute(own_w, "c", SWAP)
    far_w, far_sib_w, start = [], [], 0
    for size in CHUNKS:
        chunk = lax.ppermute(own_w[:, start : start + size], "xl", SWAP)
        far_w.append(chunk)
        far_sib_w.append(lax.ppermute(chunk, "c", SWAP))
        start += size
    head_all = lax.all_gather(heads[0], ("xl", "c"), axis=0, tiled=False)
    my_xl, my_c = lax.axis_index("xl"), lax.axis_index("c")

    def head_of(xl, c):
        return lax.dynamic_index_in_dim(head_all, xl * NC + c, 0, keepdims=False)

    own_h = heads[0]
    sib_h, far_h, far_sib_h = head_of(my_xl, 1 - my_c), head_of(1 - my_xl, my_c), head_of(1 - my_xl, 1 - my_c)

    pieces = [(own_w, own_h), (sib_w, sib_h)]
    start = 0
    for size, chunk, sib_chunk in zip(CHUNKS, far_w, far_sib_w):
        pieces.append((chunk, far_h[start : start + size]))
        pieces.append((sib_chunk, far_sib_h[start : start + size]))
        start += size

    owner = pairing[:, 0]
    live = valid == 1
    row_iota = jnp.arange(rows_dev, dtype=jnp.int32)
    same = (owner[:, None] == owner[None, :]) & (row_iota[None, :] < row_iota[:, None]) & live[None, :]
    second = jnp.sum(same.astype(jnp.int32), axis=1)
    agent_iota = jnp.arange(n_agents, dtype=jnp.int32)
    named = (agent_iota[:, None] == owner[None, :]) & live[None, :]
    picks = [(named & (second[None, :] == k)).astype(jnp.bfloat16) for k in range(2)]
    outgoing = jnp.stack(
        [jnp.dot(p, observations, preferred_element_type=jnp.float32).astype(jnp.bfloat16) for p in picks], axis=1
    )
    received = lax.all_to_all(outgoing, exchange, 0, 0, axis_index_groups=groups, tiled=True)
    visiting = scaled_rows(received.reshape(2 * n_agents, width), gain)
    answers = sum(partial_values(visiting, w, h) for w, h in pieces)
    returned = lax.all_to_all(
        answers.reshape(n_agents, 2), exchange, 0, 0, axis_index_groups=groups, tiled=True
    )
    resident = scaled_rows(observations, gain)
    own_value = sum(partial_values(resident, w, h) for w, h in pieces)
    chosen = jnp.where(second[:, None] == 0, returned[None, :, 0], returned[None, :, 1])
    opponent_value = jnp.sum(jnp.where(named.T, chosen, 0.0), axis=1)
    return own_value, opponent_value


def solution(mesh):
    wide = Mesh(mesh.devices.reshape(NZ, NXH, NY, NXL, NC), AXES)
    league, rep = AXES[:3], AXES[3:]
    return jax.shard_map(
        per_device,
        mesh=wide,
        in_specs=(
            P(AXES, None),
            P(league, None, rep),
            P(league, None),
            P(league, rep),
            P(AXES, None),
            P(AXES),
        ),
        out_specs=(P(AXES), P(AXES)),
        check_vma=False,
    )
```

```python
import functools

import jax
import jax.numpy as jnp
from jax import lax
from jax.experimental import pallas as pl
from jax.experimental.pallas import tpu as pltpu
from jax.sharding import Mesh, PartitionSpec as P

NZ, NXH, NY, NXL, NC = 8, 2, 8, 2, 2
AXES = ("z", "xh", "y", "xl", "c")
SWAP = [(0, 1), (1, 0)]
CHUNKS = (256, 256)
PAD = 8
COST_EARLY = 5
VMEM_LIMIT = 40 * 1024 * 1024


def exchange_groups():
    groups = []
    for flip in range(2):
        group = []
        for z in range(NZ):
            for xh in range(NXH):
                for y in range(NY):
                    group.append(((z * NXH + xh) * NY + y) * NXL + (xh ^ flip))
        groups.append(group)
    return groups


def hint(weight):
    return pl.CostEstimate(flops=weight * 1_000_000_000, bytes_accessed=0, transcendentals=0)


def whole(shape):
    return pl.BlockSpec(shape, lambda *_: (0,) * len(shape))


def fill_slots(owner_ref, valid_ref, rows_ref, out_ref):
    count = owner_ref.shape[1]
    agents = out_ref.shape[0]
    owner = owner_ref[...]
    live = valid_ref[...]
    owner_down = jnp.broadcast_to(owner, (count, count)).T
    live_down = jnp.broadcast_to(live, (count, count)).T
    down = lax.broadcasted_iota(jnp.int32, (count, count), 0)
    across = lax.broadcasted_iota(jnp.int32, (count, count), 1)
    earlier = (owner_down == owner) & (live_down == 1) & (down < across)
    slot = jnp.sum(earlier.astype(jnp.int32), axis=0, keepdims=True)
    agent = lax.broadcasted_iota(jnp.int32, (agents, count), 0)
    named = (agent == owner) & (live == 1)
    rows = rows_ref[...]
    for k in range(2):
        pick = (named & (slot == k)).astype(jnp.float32).astype(jnp.bfloat16)
        out_ref[:, k, :] = jnp.dot(pick, rows, preferred_element_type=jnp.float32).astype(jnp.bfloat16)


def slots_call(owner, valid, rows, agents):
    count, width = rows.shape
    return pl.pallas_call(
        fill_slots,
        out_shape=jax.ShapeDtypeStruct((agents, 2, width), jnp.bfloat16),
        compiler_params=pltpu.CompilerParams(vmem_limit_bytes=VMEM_LIMIT),
        cost_estimate=hint(200),
        name="fill_slots",
    )(owner, valid, rows)


def scaled_rows(rows, gain):
    wide = rows.astype(jnp.float32)
    squares = jnp.mean(wide * wide, axis=1, keepdims=True)
    return (wide * lax.rsqrt(squares + 1e-06) * gain).astype(jnp.bfloat16)


def partial_values(scaled, weight, head):
    hidden = jnp.dot(scaled, weight, preferred_element_type=jnp.float32)
    half = 0.5 * hidden
    return jnp.sum((half + half * jnp.tanh(half)) * head.astype(jnp.float32), axis=1, keepdims=True)


def score_near(slotted, x_ref, gain_ref, w0_ref, h0_ref, w1_ref, h1_ref, scaled_ref, value_ref):
    @pl.when(pl.program_id(0) == 0)
    def _():
        gain = gain_ref[...]
        if slotted:
            count = x_ref.shape[0]
            for k in range(2):
                scaled_ref[k * count : (k + 1) * count, :] = scaled_rows(x_ref[:, k, :], gain)
        else:
            scaled_ref[...] = scaled_rows(x_ref[...], gain)
        value_ref[...] = jnp.zeros_like(value_ref)

    scaled = scaled_ref[...]
    value_ref[...] += partial_values(scaled, w0_ref[...], h0_ref[...]) + partial_values(scaled, w1_ref[...], h1_ref[...])


def near_call(x, gain, own_w, own_h, sib_w, sib_h, slotted, step=256):
    rows = x.shape[0] * 2 if slotted else x.shape[0]
    width, units = own_w.shape
    w_spec = pl.BlockSpec((width, step), lambda j: (0, j))
    h_spec = pl.BlockSpec((1, step), lambda j: (0, j))
    return pl.pallas_call(
        functools.partial(score_near, slotted),
        grid=(units // step,),
        in_specs=[whole(x.shape), whole(gain.shape), w_spec, h_spec, w_spec, h_spec],
        out_specs=[whole((rows, width)), whole((rows, 1))],
        out_shape=[jax.ShapeDtypeStruct((rows, width), jnp.bfloat16), jax.ShapeDtypeStruct((rows, 1), jnp.float32)],
        compiler_params=pltpu.CompilerParams(vmem_limit_bytes=VMEM_LIMIT),
        cost_estimate=hint(0),
        name="score_near",
    )(x, gain, own_w, own_h, sib_w, sib_h)


def score_far(slotted, scaled_ref, near_ref, *refs):
    *chunk_refs, out_ref, value_ref = refs
    step = pl.program_id(0)

    @pl.when(step == 0)
    def _():
        value_ref[...] = near_ref[...]

    scaled = scaled_ref[...]
    total = value_ref[...]
    for w_ref, h_ref in zip(chunk_refs[::2], chunk_refs[1::2]):
        total += partial_values(scaled, w_ref[...], h_ref[0:1, :])
    value_ref[...] = total

    @pl.when(step == pl.num_programs(0) - 1)
    def _():
        if slotted:
            half = total.shape[0] // 2
            out_ref[:, 0:1] = total[:half]
            out_ref[:, 1:2] = total[half:]
        else:
            out_ref[...] = total


def far_call(scaled, near, chunks, slotted, weight, steps=2):
    rows, width = scaled.shape
    specs, args, units = [], [], 0
    for chunk in chunks:
        step = chunk.shape[1] // steps
        specs += [pl.BlockSpec((width, step), lambda j: (0, j)), pl.BlockSpec((PAD, step), lambda j: (width // PAD, j))]
        args += [chunk, chunk]
        units += chunk.shape[1]
    out = (rows // 2, 2) if slotted else (rows, 1)
    return pl.pallas_call(
        functools.partial(score_far, slotted),
        grid=(steps,),
        in_specs=[whole(scaled.shape), whole(near.shape)] + specs,
        out_specs=whole(out),
        out_shape=jax.ShapeDtypeStruct(out, jnp.float32),
        scratch_shapes=[pltpu.VMEM((rows, 1), jnp.float32)],
        compiler_params=pltpu.CompilerParams(vmem_limit_bytes=VMEM_LIMIT),
        cost_estimate=hint(weight),
        name="score_far",
    )(scaled, near, *args)


def per_device(observations, weights, gains, heads, pairing, valid):
    rows_dev, width = observations.shape
    n_agents = NZ * NXH * NY
    groups = exchange_groups()
    own_w = weights[0]
    exchange = ("z", "xh", "y", "xl")

    def pack(start, stop):
        head = jnp.broadcast_to(heads[:, start:stop], (PAD, stop - start))
        return jnp.concatenate([own_w[:, start:stop], head], axis=0)

    first = lax.ppermute(pack(0, CHUNKS[0]), "xl", SWAP)
    second = lax.ppermute(pack(CHUNKS[0], sum(CHUNKS)), "xl", SWAP)
    outgoing = slots_call(pairing.reshape(1, rows_dev), valid.reshape(1, rows_dev), observations, n_agents)
    near_w, near_h, outgoing = lax.optimization_barrier((own_w, heads, outgoing))
    sib_w = lax.ppermute(near_w, "c", SWAP)
    sib_h = lax.ppermute(near_h, "c", SWAP)
    early = (first, lax.ppermute(first, "c", SWAP))
    own_scaled, own = near_call(observations, gains, own_w, heads, sib_w, sib_h, False)
    own = far_call(own_scaled, own, early, False, 0)
    second, own, own_scaled = lax.optimization_barrier((second, own, own_scaled))
    late = (second, lax.ppermute(second, "c", SWAP))

    received = lax.all_to_all(outgoing, exchange, 0, 0, axis_index_groups=groups, tiled=True)
    visit_scaled, visit = near_call(received, gains, own_w, heads, sib_w, sib_h, True)
    visit = far_call(visit_scaled, visit, early, False, COST_EARLY)
    answers = far_call(visit_scaled, visit, late, True, 0)
    returned = lax.all_to_all(answers, exchange, 0, 0, axis_index_groups=groups, tiled=True)
    own_value = far_call(own_scaled, own, late, False, 0)[:, 0]

    owner = pairing[:, 0]
    is_live = valid == 1
    row_iota = jnp.arange(rows_dev, dtype=jnp.int32)
    same = (owner[:, None] == owner[None, :]) & (row_iota[None, :] < row_iota[:, None]) & is_live[None, :]
    second = jnp.sum(same.astype(jnp.int32), axis=1)
    agent_iota = jnp.arange(n_agents, dtype=jnp.int32)
    chosen = jnp.where(second[:, None] == 0, returned[None, :, 0], returned[None, :, 1])
    named = (owner[:, None] == agent_iota[None, :]) & is_live[:, None]
    opponent_value = jnp.sum(jnp.where(named, chosen, 0.0), axis=1)
    return own_value, opponent_value


def solution(mesh):
    wide = Mesh(mesh.devices.reshape(NZ, NXH, NY, NXL, NC), AXES)
    league, rep = AXES[:3], AXES[3:]
    return jax.shard_map(
        per_device,
        mesh=wide,
        in_specs=(
            P(AXES, None),
            P(league, None, rep),
            P(league, None),
            P(league, rep),
            P(AXES, None),
            P(AXES),
        ),
        out_specs=(P(AXES), P(AXES)),
        check_vma=False,
    )
```

```python
import functools

import jax
import jax.numpy as jnp
from jax import lax
from jax.experimental import pallas as pl
from jax.experimental.pallas import tpu as pltpu
from jax.sharding import Mesh, PartitionSpec as P

NZ, NXH, NY, NXL, NC = 8, 2, 8, 2, 2
AXES = ("z", "xh", "y", "xl", "c")
SWAP = [(0, 1), (1, 0)]
COST_FIRST = 5
VMEM_LIMIT = 40 * 1024 * 1024


def exchange_groups():
    groups = []
    for flip in range(2):
        group = []
        for z in range(NZ):
            for xh in range(NXH):
                for y in range(NY):
                    group.append(((z * NXH + xh) * NY + y) * NXL + (xh ^ flip))
        groups.append(group)
    return groups


def hint(weight):
    return pl.CostEstimate(flops=weight * 1_000_000_000, bytes_accessed=0, transcendentals=0)


def whole(shape):
    return pl.BlockSpec(shape, lambda *_: (0,) * len(shape))


def fill_slots(owner_ref, valid_ref, rows_ref, out_ref, slot_ref):
    count = owner_ref.shape[1]
    agents = out_ref.shape[0]
    owner = owner_ref[...]
    live = valid_ref[...]
    owner_down = jnp.broadcast_to(owner, (count, count)).T
    live_down = jnp.broadcast_to(live, (count, count)).T
    down = lax.broadcasted_iota(jnp.int32, (count, count), 0)
    across = lax.broadcasted_iota(jnp.int32, (count, count), 1)
    earlier = (owner_down == owner) & (live_down == 1) & (down < across)
    slot = jnp.sum(earlier.astype(jnp.int32), axis=0, keepdims=True)
    agent = lax.broadcasted_iota(jnp.int32, (agents, count), 0)
    named = (agent == owner) & (live == 1)
    slot_ref[...] = jnp.where(live == 1, slot, 2)
    rows = rows_ref[...]
    for k in range(2):
        pick = (named & (slot == k)).astype(jnp.float32).astype(jnp.bfloat16)
        out_ref[:, k, :] = jnp.dot(pick, rows, preferred_element_type=jnp.float32).astype(jnp.bfloat16)


def slots_call(owner, valid, rows, agents):
    count, width = rows.shape
    return pl.pallas_call(
        fill_slots,
        out_shape=[
            pltpu.HBM((agents, 2, width), jnp.bfloat16),
            jax.ShapeDtypeStruct((1, count), jnp.int32),
        ],
        compiler_params=pltpu.CompilerParams(vmem_limit_bytes=VMEM_LIMIT),
        cost_estimate=hint(200),
        name="fill_slots",
    )(owner, valid, rows)


def pick_answers(returned_ref, owner_ref, slot_ref, out_ref):
    agents, count = returned_ref.shape[0], owner_ref.shape[1]
    slot = slot_ref[...]
    answer = jnp.where(slot == 0, returned_ref[:, 0:1], returned_ref[:, 1:2])
    agent = lax.broadcasted_iota(jnp.int32, (agents, count), 0)
    named = (agent == owner_ref[...]) & (slot < 2)
    out_ref[...] = jnp.sum(jnp.where(named, answer, 0.0), axis=0, keepdims=True)


def pick_call(returned, owner, slot):
    return pl.pallas_call(
        pick_answers,
        out_shape=jax.ShapeDtypeStruct(owner.shape, jnp.float32),
        cost_estimate=hint(0),
        name="pick_answers",
    )(returned, owner, slot)


def scaled_rows(rows, gain):
    wide = rows.astype(jnp.float32)
    squares = jnp.mean(wide * wide, axis=1, keepdims=True)
    return (wide * lax.rsqrt(squares + 1e-06) * gain).astype(jnp.bfloat16)


def partial_values(scaled, weight, head):
    hidden = jnp.dot(scaled, weight, preferred_element_type=jnp.float32)
    half = 0.5 * hidden
    return jnp.sum((half + half * jnp.tanh(half)) * head.astype(jnp.float32), axis=1, keepdims=True)


def score_own(x_ref, gain_ref, w_ref, h_ref, scaled_ref, value_ref):
    @pl.when(pl.program_id(0) == 0)
    def _():
        scaled_ref[...] = scaled_rows(x_ref[...], gain_ref[...])
        value_ref[...] = jnp.zeros_like(value_ref)

    value_ref[...] += partial_values(scaled_ref[...], w_ref[...], h_ref[...])


def score_first(x_ref, gain_ref, own_ref, own_near_ref, w0_ref, h0_ref, w1_ref, h1_ref, scaled_ref, visit_out, own_out):
    @pl.when(pl.program_id(0) == 0)
    def _():
        gain = gain_ref[...]
        count = x_ref.shape[0]
        for k in range(2):
            scaled_ref[k * count : (k + 1) * count, :] = scaled_rows(x_ref[:, k, :], gain)
        visit_out[...] = jnp.zeros_like(visit_out)
        own_out[...] = own_near_ref[...]

    scaled = scaled_ref[...]
    visit_out[...] += partial_values(scaled, w0_ref[...], h0_ref[...]) + partial_values(scaled, w1_ref[...], h1_ref[0:1])
    own_out[...] += partial_values(own_ref[...], w1_ref[...], h1_ref[0:1])


def score_last(
    visit_ref, own_ref, visit_near_ref, own_near_ref, w0_ref, h0_ref, w1_ref, h1_ref, answer_out, value_out, visit_total, own_total
):
    @pl.when(pl.program_id(0) == 0)
    def _():
        visit_total[...] = visit_near_ref[...]
        own_total[...] = own_near_ref[...]

    for rows_ref, total in ((visit_ref, visit_total), (own_ref, own_total)):
        rows = rows_ref[...]
        total[...] += partial_values(rows, w0_ref[...], h0_ref[...]) + partial_values(rows, w1_ref[...], h1_ref[1:2])

    @pl.when(pl.program_id(0) == pl.num_programs(0) - 1)
    def _():
        half = answer_out.shape[0]
        answer_out[:, 0:1] = visit_total[:half]
        answer_out[:, 1:2] = visit_total[half:]
        value_out[...] = jnp.broadcast_to(own_total[...], (half, half)).T[0:1]


def score_call(body, fixed, weights, heads, outs, scratch, weight, step=256):
    width, units = weights[0].shape
    specs, args = [whole(x.shape) for x in fixed], list(fixed)
    for w, h in zip(weights, heads):
        specs += [pl.BlockSpec((width, step), lambda j: (0, j)), pl.BlockSpec((h.shape[0], step), lambda j: (0, j))]
        args += [w, h]
    return pl.pallas_call(
        body,
        grid=(units // step,),
        in_specs=specs,
        out_specs=[whole(shape) for shape, _ in outs],
        out_shape=[jax.ShapeDtypeStruct(*out) for out in outs],
        scratch_shapes=[pltpu.VMEM(shape, jnp.float32) for shape in scratch],
        compiler_params=pltpu.CompilerParams(vmem_limit_bytes=VMEM_LIMIT),
        cost_estimate=hint(weight),
        name=body.__name__,
    )(*args)


def per_device(observations, weights, gains, heads, pairing, valid):
    rows_dev, width = observations.shape
    n_agents = NZ * NXH * NY
    groups = exchange_groups()
    own_w = weights[0]
    exchange = ("z", "xh", "y", "xl")

    far_w = lax.ppermute(own_w, "xl", SWAP)
    owner = pairing.reshape(1, rows_dev)
    outgoing, slot = slots_call(owner, valid.reshape(1, rows_dev), observations, n_agents)
    near_h, slot = lax.optimization_barrier((heads, slot))
    received = lax.all_to_all(outgoing, exchange, 0, 0, axis_index_groups=groups, tiled=True)
    sib_h = lax.ppermute(near_h, "c", SWAP)
    near_w, sib_h = lax.optimization_barrier((own_w, sib_h))
    sib_w = lax.ppermute(near_w, "c", SWAP)
    far_h = lax.ppermute(jnp.concatenate([heads, sib_h], axis=0), "xl", SWAP)
    f32, bf16 = jnp.float32, jnp.bfloat16
    visits = 2 * n_agents
    own_scaled, own = score_call(
        score_own, (observations, gains), (own_w,), (heads,), [((rows_dev, width), bf16), ((rows_dev, 1), f32)], [], 0
    )
    received, far_w, far_h, own_scaled, own = lax.optimization_barrier((received, far_w, far_h, own_scaled, own))
    far_sib_w = lax.ppermute(far_w, "c", SWAP)
    visit_scaled, visit, own = score_call(
        score_first,
        (received, gains, own_scaled, own),
        (own_w, far_w),
        (heads, far_h),
        [((visits, width), bf16), ((visits, 1), f32), ((rows_dev, 1), f32)],
        [],
        COST_FIRST,
    )
    answers, own_value = score_call(
        score_last,
        (visit_scaled, own_scaled, visit, own),
        (sib_w, far_sib_w),
        (sib_h, far_h),
        [((n_agents, 2), f32), ((1, rows_dev), f32)],
        [(visits, 1), (rows_dev, 1)],
        0,
    )
    returned = lax.all_to_all(answers, exchange, 0, 0, axis_index_groups=groups, tiled=True)

    opponent_value = pick_call(returned, owner, slot)
    return own_value.reshape(rows_dev), opponent_value.reshape(rows_dev)


def solution(mesh):
    wide = Mesh(mesh.devices.reshape(NZ, NXH, NY, NXL, NC), AXES)
    league, rep = AXES[:3], AXES[3:]
    return jax.shard_map(
        per_device,
        mesh=wide,
        in_specs=(
            P(AXES, None),
            P(league, None, rep),
            P(league, None),
            P(league, rep),
            P(AXES, None),
            P(AXES),
        ),
        out_specs=(P(AXES), P(AXES)),
        check_vma=False,
    )
```

```python
import functools

import jax
import jax.numpy as jnp
from jax import lax
from jax.experimental import pallas as pl
from jax.experimental.pallas import tpu as pltpu
from jax.sharding import Mesh, PartitionSpec as P

NZ, NXH, NY, NXL, NC = 8, 2, 8, 2, 2
AXES = ("z", "xh", "y", "xl", "c")
SWAP = [(0, 1), (1, 0)]
COST_FIRST = 5
SLOTS_VMEM = 60 * 1024 * 1024
SCORE_VMEM = 16 * 1024 * 1024
REST_VMEM = 32 * 1024 * 1024
STEP = 256


def exchange_groups():
    groups = []
    for flip in range(2):
        group = []
        for z in range(NZ):
            for xh in range(NXH):
                for y in range(NY):
                    group.append(((z * NXH + xh) * NY + y) * NXL + (xh ^ flip))
        groups.append(group)
    return groups


def hint(weight):
    return pl.CostEstimate(flops=weight * 1_000_000_000, bytes_accessed=0, transcendentals=0)


def fill_slots(owner_hbm, valid_hbm, rows_hbm, out_ref, slot_ref, owner_ref, valid_ref, rows_ref, arrived):
    pairs = ((owner_hbm, owner_ref), (valid_hbm, valid_ref), (rows_hbm, rows_ref))
    copies = [pltpu.make_async_copy(src, dst, arrived.at[i]) for i, (src, dst) in enumerate(pairs)]
    for copy in copies:
        copy.start()
    count = owner_ref.shape[1]
    agents = out_ref.shape[0]
    copies[0].wait()
    copies[1].wait()
    owner = owner_ref[...]
    live = valid_ref[...]
    owner_down = jnp.broadcast_to(owner, (count, count)).T
    live_down = jnp.broadcast_to(live, (count, count)).T
    down = lax.broadcasted_iota(jnp.int32, (count, count), 0)
    across = lax.broadcasted_iota(jnp.int32, (count, count), 1)
    earlier = (owner_down == owner) & (live_down == 1) & (down < across)
    slot = jnp.sum(earlier.astype(jnp.int32), axis=0, keepdims=True)
    agent = lax.broadcasted_iota(jnp.int32, (agents, count), 0)
    named = (agent == owner) & (live == 1)
    slot_ref[...] = jnp.where(live == 1, slot, 2)
    copies[2].wait()
    rows = rows_ref[...]
    for k in range(2):
        pick = (named & (slot == k)).astype(jnp.float32).astype(jnp.bfloat16)
        out_ref[:, k, :] = jnp.dot(pick, rows, preferred_element_type=jnp.float32).astype(jnp.bfloat16)


def slots_call(owner, valid, rows, agents):
    count, width = rows.shape
    return pl.pallas_call(
        fill_slots,
        in_specs=[pl.BlockSpec(memory_space=pltpu.HBM)] * 3,
        out_shape=[
            pltpu.HBM((agents, 2, width), jnp.bfloat16),
            jax.ShapeDtypeStruct((1, count), jnp.int32),
        ],
        scratch_shapes=[
            pltpu.VMEM(owner.shape, owner.dtype),
            pltpu.VMEM(valid.shape, valid.dtype),
            pltpu.VMEM(rows.shape, rows.dtype),
            pltpu.SemaphoreType.DMA((3,)),
        ],
        compiler_params=pltpu.CompilerParams(vmem_limit_bytes=SLOTS_VMEM),
        cost_estimate=hint(200),
        name="fill_slots",
    )(owner, valid, rows)


def pick_answers(returned_ref, owner_ref, slot_ref, out_ref):
    agents, count = returned_ref.shape[0], owner_ref.shape[1]
    slot = slot_ref[...]
    answer = jnp.where(slot == 0, returned_ref[:, 0:1], returned_ref[:, 1:2])
    agent = lax.broadcasted_iota(jnp.int32, (agents, count), 0)
    named = (agent == owner_ref[...]) & (slot < 2)
    out_ref[...] = jnp.sum(jnp.where(named, answer, 0.0), axis=0, keepdims=True)


def pick_call(returned, owner, slot):
    return pl.pallas_call(
        pick_answers,
        out_shape=jax.ShapeDtypeStruct(owner.shape, jnp.float32),
        cost_estimate=hint(0),
        name="pick_answers",
    )(returned, owner, slot)


def scaled_rows(rows, gain):
    wide = rows.astype(jnp.float32)
    squares = jnp.mean(wide * wide, axis=1, keepdims=True)
    return (wide * lax.rsqrt(squares + 1e-06) * gain).astype(jnp.bfloat16)


def values(rows, weight, head):
    hidden = jnp.dot(rows, weight, preferred_element_type=jnp.float32)
    half = 0.5 * hidden
    return jnp.sum((half + half * jnp.tanh(half)) * head, axis=1, keepdims=True)


def scale_own(x_ref, gain_ref, scaled_ref):
    scaled_ref[...] = scaled_rows(x_ref[...], gain_ref[...])


def scale_visit(x_ref, gain_ref, scaled_ref):
    count = x_ref.shape[0]
    for k in range(2):
        scaled_ref[k * count : (k + 1) * count, :] = scaled_rows(x_ref[:, k, :], gain_ref[...])


def score_rows(
    visit_ref, own_hbm, w0_hbm, h0_ref, w1_hbm, h1_ref, w2_hbm, w3_hbm, h23_ref,
    answer_out, value_out, own_ref, blocks_ref, arrived,
):
    weights = (w0_hbm, w1_hbm, w2_hbm, w3_hbm)
    copies = [pltpu.make_async_copy(own_hbm, own_ref, arrived.at[0])]
    jobs = []
    for n, w_hbm in enumerate(weights):
        for start in range(0, w_hbm.shape[1], STEP):
            i = len(jobs)
            jobs.append((n, start))
            copies.append(pltpu.make_async_copy(w_hbm.at[:, pl.ds(start, STEP)], blocks_ref.at[i], arrived.at[i + 1]))
    for copy in copies:
        copy.start()
    heads = [h0_ref[...].astype(jnp.float32), h1_ref[...].astype(jnp.float32)]
    far_heads = h23_ref[...].astype(jnp.float32)
    heads += [far_heads[0:1], far_heads[1:2]]
    copies[0].wait()
    visit = jnp.zeros((visit_ref.shape[0], 1), jnp.float32)
    own = jnp.zeros((own_ref.shape[0], 1), jnp.float32)
    for i, (n, start) in enumerate(jobs):
        copies[i + 1].wait()
        block, head = blocks_ref[i], heads[n][:, start : start + STEP]
        visit += values(visit_ref[...], block, head)
        own += values(own_ref[...], block, head)
    half = answer_out.shape[0]
    answer_out[:, 0:1] = visit[:half]
    answer_out[:, 1:2] = visit[half:]
    value_out[...] = jnp.broadcast_to(own, (half, half)).T[0:1]


def score_call(body, operands, outs, weight, hbm=(), scratch=(), limit=0):
    vmem, anywhere = pl.BlockSpec(memory_space=pltpu.VMEM), pl.BlockSpec(memory_space=pl.ANY)
    return pl.pallas_call(
        body,
        in_specs=[anywhere if i in hbm else vmem for i in range(len(operands))],
        out_shape=outs,
        scratch_shapes=scratch,
        compiler_params=pltpu.CompilerParams(vmem_limit_bytes=limit or SCORE_VMEM),
        cost_estimate=hint(weight),
        name=body.__name__,
    )(*operands)


def per_device(observations, weights, gains, heads, pairing, valid):
    rows_dev, width = observations.shape
    n_agents = NZ * NXH * NY
    groups = exchange_groups()
    own_w = weights[0]
    exchange = ("z", "xh", "y", "xl")

    far_w = lax.ppermute(own_w, "xl", SWAP)
    owner = pairing.reshape(1, rows_dev)
    outgoing, slot = slots_call(owner, valid.reshape(1, rows_dev), observations, n_agents)
    near_h, slot = lax.optimization_barrier((heads, slot))
    received = lax.all_to_all(outgoing, exchange, 0, 0, axis_index_groups=groups, tiled=True)
    sib_h = lax.ppermute(near_h, "c", SWAP)
    near_w, sib_h = lax.optimization_barrier((own_w, sib_h))
    sib_w = lax.ppermute(near_w, "c", SWAP)
    far_h = lax.ppermute(jnp.concatenate([heads, sib_h], axis=0), "xl", SWAP)
    f32, bf16 = jnp.float32, jnp.bfloat16
    visits, units = 2 * n_agents, own_w.shape[1]
    shape = jax.ShapeDtypeStruct
    own_scaled = score_call(scale_own, (observations, gains), pltpu.HBM((rows_dev, width), bf16), 0)
    received, far_h, own_scaled = lax.optimization_barrier((received, far_h, own_scaled))
    far_sib_w = lax.ppermute(far_w, "c", SWAP)
    visit_scaled = score_call(scale_visit, (received, gains), shape((visits, width), bf16), COST_FIRST)
    blocks = 4 * units // STEP
    answers, own_value = score_call(
        score_rows,
        (visit_scaled, own_scaled, own_w, heads, sib_w, sib_h, far_w, far_sib_w, far_h),
        [shape((n_agents, 2), f32), shape((1, rows_dev), f32)],
        0,
        hbm=(1, 2, 4, 6, 7),
        scratch=[
            pltpu.VMEM((rows_dev, width), bf16),
            pltpu.VMEM((blocks, width, STEP), bf16),
            pltpu.SemaphoreType.DMA((blocks + 1,)),
        ],
        limit=REST_VMEM,
    )
    returned = lax.all_to_all(answers, exchange, 0, 0, axis_index_groups=groups, tiled=True)

    opponent_value = pick_call(returned, owner, slot)
    return own_value.reshape(rows_dev), opponent_value.reshape(rows_dev)


def solution(mesh):
    wide = Mesh(mesh.devices.reshape(NZ, NXH, NY, NXL, NC), AXES)
    league, rep = AXES[:3], AXES[3:]
    return jax.shard_map(
        per_device,
        mesh=wide,
        in_specs=(
            P(AXES, None),
            P(league, None, rep),
            P(league, None),
            P(league, rep),
            P(AXES, None),
            P(AXES),
        ),
        out_specs=(P(AXES), P(AXES)),
        check_vma=False,
    )
```

```python
import functools

import jax
import jax.numpy as jnp
from jax import lax
from jax.experimental import pallas as pl
from jax.experimental.pallas import tpu as pltpu
from jax.sharding import Mesh, PartitionSpec as P

NZ, NXH, NY, NXL, NC = 8, 2, 8, 2, 2
AXES = ("z", "xh", "y", "xl", "c")
SWAP = [(0, 1), (1, 0)]
COST_FIRST = 5
SLOTS_VMEM = 60 * 1024 * 1024
SCORE_VMEM = 16 * 1024 * 1024
REST_VMEM = 32 * 1024 * 1024
STEP = 256
SCALE_AGENTS = 32


def exchange_groups():
    groups = []
    for flip in range(2):
        group = []
        for z in range(NZ):
            for xh in range(NXH):
                for y in range(NY):
                    group.append(((z * NXH + xh) * NY + y) * NXL + (xh ^ flip))
        groups.append(group)
    return groups


def hint(weight):
    return pl.CostEstimate(flops=weight * 1_000_000_000, bytes_accessed=0, transcendentals=0)


def fill_slots(owner_hbm, valid_hbm, rows_hbm, out_ref, slot_ref, owner_ref, valid_ref, rows_ref, arrived):
    pairs = ((owner_hbm, owner_ref), (valid_hbm, valid_ref), (rows_hbm, rows_ref))
    copies = [pltpu.make_async_copy(src, dst, arrived.at[i]) for i, (src, dst) in enumerate(pairs)]
    for copy in copies:
        copy.start()
    count = owner_ref.shape[1]
    agents = out_ref.shape[0]
    copies[0].wait()
    copies[1].wait()
    owner = owner_ref[...]
    live = valid_ref[...]
    owner_down = jnp.broadcast_to(owner, (count, count)).T
    live_down = jnp.broadcast_to(live, (count, count)).T
    down = lax.broadcasted_iota(jnp.int32, (count, count), 0)
    across = lax.broadcasted_iota(jnp.int32, (count, count), 1)
    earlier = (owner_down == owner) & (live_down == 1) & (down < across)
    slot = jnp.sum(earlier.astype(jnp.int32), axis=0, keepdims=True)
    slot_ref[...] = jnp.where(live == 1, slot, 2)
    place = lax.broadcasted_iota(jnp.int32, (2 * agents, count), 0)
    pick = ((place == 2 * owner + slot) & (live == 1)).astype(jnp.float32).astype(jnp.bfloat16)
    copies[2].wait()
    out = jnp.dot(pick, rows_ref[...], preferred_element_type=jnp.float32).astype(jnp.bfloat16)
    out_ref[...] = out.reshape(out_ref.shape)


def slots_call(owner, valid, rows, agents):
    count, width = rows.shape
    return pl.pallas_call(
        fill_slots,
        in_specs=[pl.BlockSpec(memory_space=pltpu.HBM)] * 3,
        out_shape=[
            pltpu.HBM((agents, 2, width), jnp.bfloat16),
            jax.ShapeDtypeStruct((1, count), jnp.int32),
        ],
        scratch_shapes=[
            pltpu.VMEM(owner.shape, owner.dtype),
            pltpu.VMEM(valid.shape, valid.dtype),
            pltpu.VMEM(rows.shape, rows.dtype),
            pltpu.SemaphoreType.DMA((3,)),
        ],
        compiler_params=pltpu.CompilerParams(vmem_limit_bytes=SLOTS_VMEM),
        cost_estimate=hint(200),
        name="fill_slots",
    )(owner, valid, rows)


def pick_answers(returned_ref, owner_ref, slot_ref, out_ref):
    agents, count = returned_ref.shape[0], owner_ref.shape[1]
    slot = slot_ref[...]
    answer = jnp.where(slot == 0, returned_ref[:, 0:1], returned_ref[:, 1:2])
    agent = lax.broadcasted_iota(jnp.int32, (agents, count), 0)
    named = (agent == owner_ref[...]) & (slot < 2)
    out_ref[...] = jnp.sum(jnp.where(named, answer, 0.0), axis=0, keepdims=True)


def pick_call(returned, owner, slot):
    return pl.pallas_call(
        pick_answers,
        out_shape=jax.ShapeDtypeStruct(owner.shape, jnp.float32),
        cost_estimate=hint(0),
        name="pick_answers",
    )(returned, owner, slot)


def scaled_rows(rows, gain):
    wide = rows.astype(jnp.float32)
    squares = jnp.mean(wide * wide, axis=1, keepdims=True)
    return (wide * lax.rsqrt(squares + 1e-06) * gain).astype(jnp.bfloat16)


def values(rows, weight, head):
    hidden = jnp.dot(rows, weight, preferred_element_type=jnp.float32)
    half = 0.5 * hidden
    return jnp.sum((half + half * jnp.tanh(half)) * head, axis=1, keepdims=True)


def scale_own(x_ref, gain_ref, scaled_ref):
    scaled_ref[...] = scaled_rows(x_ref[...], gain_ref[...])


def fetch_blocks(weights, blocks_ref, arrived):
    jobs = []
    for n, w_hbm in enumerate(weights):
        for start in range(0, w_hbm.shape[1], STEP):
            i = len(jobs)
            copy = pltpu.make_async_copy(w_hbm.at[:, pl.ds(start, STEP)], blocks_ref.at[i], arrived.at[i])
            copy.start()
            jobs.append((copy, n, start))
    return jobs


def add_blocks(total, rows_ref, jobs, blocks_ref, heads):
    for i, (copy, n, start) in enumerate(jobs):
        copy.wait()
        total += values(rows_ref[...], blocks_ref[i], heads[n][:, start : start + STEP])
    return total


def score_first(
    x_hbm, gain_ref, own_hbm, w_hbm, h_ref, scaled_ref, value_ref, x_ref, blocks_ref, rows_here, arrived
):
    agents, slots, _ = x_ref.shape
    visits, owns = agents * slots, own_hbm.shape[0]
    visit_copy = pltpu.make_async_copy(x_hbm, x_ref, rows_here.at[0])
    own_copy = pltpu.make_async_copy(own_hbm, scaled_ref.at[pl.ds(visits, owns), :], rows_here.at[1])
    visit_copy.start()
    jobs = fetch_blocks((w_hbm,), blocks_ref, arrived)
    own_copy.start()
    gain = gain_ref[...]
    heads = (h_ref[...].astype(jnp.float32)[0:1],)
    visit_copy.wait()
    for start in range(0, agents, SCALE_AGENTS):
        rows = x_ref[start : start + SCALE_AGENTS].reshape(SCALE_AGENTS * slots, gain.shape[1])
        scaled_ref[start * slots : (start + SCALE_AGENTS) * slots, :] = scaled_rows(rows, gain)
    own_copy.wait()
    value_ref[...] = add_blocks(jnp.zeros(value_ref.shape, jnp.float32), scaled_ref, jobs, blocks_ref, heads)


def score_last(
    scaled_ref, near_ref, w0_hbm, h0_ref, w1_hbm, h1_ref, w2_hbm, h2_ref, answer_out, value_out, total_ref, blocks_ref, arrived
):
    jobs = fetch_blocks((w0_hbm, w1_hbm, w2_hbm), blocks_ref, arrived)
    heads = (h0_ref[...].astype(jnp.float32), h1_ref[...].astype(jnp.float32), h2_ref[...].astype(jnp.float32)[1:2])
    total = add_blocks(near_ref[...], scaled_ref, jobs, blocks_ref, heads)
    total_ref[...] = total
    agents, slots = answer_out.shape
    for k in range(slots):
        answer_out[:, k : k + 1] = total_ref[pl.ds(k, agents, stride=slots), :]
    owns = value_out.shape[1]
    value_out[...] = jnp.broadcast_to(total[agents * slots :], (owns, owns)).T[0:1]


def score_call(body, operands, outs, weight, hbm=(), scratch=(), limit=0):
    vmem, anywhere = pl.BlockSpec(memory_space=pltpu.VMEM), pl.BlockSpec(memory_space=pl.ANY)
    return pl.pallas_call(
        body,
        in_specs=[anywhere if i in hbm else vmem for i in range(len(operands))],
        out_shape=outs,
        scratch_shapes=scratch,
        compiler_params=pltpu.CompilerParams(vmem_limit_bytes=limit or SCORE_VMEM),
        cost_estimate=hint(weight),
        name=body.__name__,
    )(*operands)


def per_device(observations, weights, gains, heads, pairing, valid):
    rows_dev, width = observations.shape
    n_agents = NZ * NXH * NY
    groups = exchange_groups()
    own_w = weights[0]
    exchange = ("z", "xh", "y", "xl")

    far_w = lax.ppermute(own_w, "xl", SWAP)
    owner = pairing.reshape(1, rows_dev)
    outgoing, slot = slots_call(owner, valid.reshape(1, rows_dev), observations, n_agents)
    near_h, slot = lax.optimization_barrier((heads, slot))
    received = lax.all_to_all(outgoing, exchange, 0, 0, axis_index_groups=groups, tiled=True)
    sib_h = lax.ppermute(near_h, "c", SWAP)
    near_w, sib_h = lax.optimization_barrier((own_w, sib_h))
    sib_w = lax.ppermute(near_w, "c", SWAP)
    far_h = lax.ppermute(jnp.concatenate([heads, sib_h], axis=0), "xl", SWAP)
    f32, bf16 = jnp.float32, jnp.bfloat16
    visits, units = 2 * n_agents, own_w.shape[1]
    shape = jax.ShapeDtypeStruct
    own_scaled = score_call(scale_own, (observations, gains), pltpu.HBM((rows_dev, width), bf16), 0)
    far_w, far_h, own_scaled = lax.optimization_barrier((far_w, far_h, own_scaled))
    far_sib_w = lax.ppermute(far_w, "c", SWAP)
    blocks = units // STEP
    scaled, near = score_call(
        score_first,
        (received, gains, own_scaled, far_w, far_h),
        [shape((visits + rows_dev, width), bf16), shape((visits + rows_dev, 1), f32)],
        COST_FIRST,
        hbm=(0, 2, 3),
        scratch=[
            pltpu.VMEM(received.shape, bf16),
            pltpu.VMEM((blocks, width, STEP), bf16),
            pltpu.SemaphoreType.DMA((2,)),
            pltpu.SemaphoreType.DMA((blocks,)),
        ],
        limit=REST_VMEM,
    )
    answers, own_value = score_call(
        score_last,
        (scaled, near, own_w, heads, sib_w, sib_h, far_sib_w, far_h),
        [shape((n_agents, 2), f32), shape((1, rows_dev), f32)],
        0,
        hbm=(2, 4, 6),
        scratch=[
            pltpu.VMEM((visits + rows_dev, 1), f32),
            pltpu.VMEM((3 * blocks, width, STEP), bf16),
            pltpu.SemaphoreType.DMA((3 * blocks,)),
        ],
        limit=REST_VMEM,
    )
    returned = lax.all_to_all(answers, exchange, 0, 0, axis_index_groups=groups, tiled=True)

    opponent_value = pick_call(returned, owner, slot)
    return own_value.reshape(rows_dev), opponent_value.reshape(rows_dev)


def solution(mesh):
    wide = Mesh(mesh.devices.reshape(NZ, NXH, NY, NXL, NC), AXES)
    league, rep = AXES[:3], AXES[3:]
    return jax.shard_map(
        per_device,
        mesh=wide,
        in_specs=(
            P(AXES, None),
            P(league, None, rep),
            P(league, None),
            P(league, rep),
            P(AXES, None),
            P(AXES),
        ),
        out_specs=(P(AXES), P(AXES)),
        check_vma=False,
    )
```

```python
import functools

import jax
import jax.numpy as jnp
from jax import lax
from jax.experimental import pallas as pl
from jax.experimental.pallas import tpu as pltpu
from jax.sharding import Mesh, PartitionSpec as P

NZ, NXH, NY, NXL, NC = 8, 2, 8, 2, 2
AXES = ("z", "xh", "y", "xl", "c")
SWAP = [(0, 1), (1, 0)]
COST_FIRST = 5
SLOTS_VMEM = 60 * 1024 * 1024
SCORE_VMEM = 16 * 1024 * 1024
REST_VMEM = 32 * 1024 * 1024
STEP = 512
SCALE_AGENTS = 32


def exchange_groups():
    groups = []
    for flip in range(2):
        group = []
        for z in range(NZ):
            for xh in range(NXH):
                for y in range(NY):
                    group.append(((z * NXH + xh) * NY + y) * NXL + (xh ^ flip))
        groups.append(group)
    return groups


def hint(weight):
    return pl.CostEstimate(flops=weight * 1_000_000_000, bytes_accessed=0, transcendentals=0)


def fill_slots(owner_hbm, valid_hbm, rows_hbm, out_ref, slot_ref, owner_ref, valid_ref, rows_ref, arrived):
    pairs = ((owner_hbm, owner_ref), (valid_hbm, valid_ref), (rows_hbm, rows_ref))
    copies = [pltpu.make_async_copy(src, dst, arrived.at[i]) for i, (src, dst) in enumerate(pairs)]
    for copy in copies:
        copy.start()
    count = owner_ref.shape[1]
    agents = out_ref.shape[0]
    copies[0].wait()
    copies[1].wait()
    owner = owner_ref[...]
    live = valid_ref[...]
    owner_down = jnp.broadcast_to(owner, (count, count)).T
    live_down = jnp.broadcast_to(live, (count, count)).T
    down = lax.broadcasted_iota(jnp.int32, (count, count), 0)
    across = lax.broadcasted_iota(jnp.int32, (count, count), 1)
    earlier = (owner_down == owner) & (live_down == 1) & (down < across)
    slot = jnp.sum(earlier.astype(jnp.int32), axis=0, keepdims=True)
    slot_ref[...] = jnp.where(live == 1, slot, 2)
    place = lax.broadcasted_iota(jnp.int32, (2 * agents, count), 0)
    pick = ((place == 2 * owner + slot) & (live == 1)).astype(jnp.float32).astype(jnp.bfloat16)
    copies[2].wait()
    out = jnp.dot(pick, rows_ref[...], preferred_element_type=jnp.float32).astype(jnp.bfloat16)
    out_ref[...] = out.reshape(out_ref.shape)


def slots_call(owner, valid, rows, agents):
    count, width = rows.shape
    return pl.pallas_call(
        fill_slots,
        in_specs=[pl.BlockSpec(memory_space=pltpu.HBM)] * 3,
        out_shape=[
            pltpu.HBM((agents, 2, width), jnp.bfloat16),
            jax.ShapeDtypeStruct((1, count), jnp.int32),
        ],
        scratch_shapes=[
            pltpu.VMEM(owner.shape, owner.dtype),
            pltpu.VMEM(valid.shape, valid.dtype),
            pltpu.VMEM(rows.shape, rows.dtype),
            pltpu.SemaphoreType.DMA((3,)),
        ],
        compiler_params=pltpu.CompilerParams(vmem_limit_bytes=SLOTS_VMEM),
        cost_estimate=hint(200),
        name="fill_slots",
    )(owner, valid, rows)


def pick_answers(returned_ref, owner_ref, slot_ref, out_ref):
    agents, count = returned_ref.shape[0], owner_ref.shape[1]
    slot = slot_ref[...]
    answer = jnp.where(slot == 0, returned_ref[:, 0:1], returned_ref[:, 1:2])
    agent = lax.broadcasted_iota(jnp.int32, (agents, count), 0)
    named = (agent == owner_ref[...]) & (slot < 2)
    out_ref[...] = jnp.sum(jnp.where(named, answer, 0.0), axis=0, keepdims=True)


def pick_call(returned, owner, slot):
    return pl.pallas_call(
        pick_answers,
        out_shape=jax.ShapeDtypeStruct(owner.shape, jnp.float32),
        cost_estimate=hint(0),
        name="pick_answers",
    )(returned, owner, slot)


def scaled_rows(rows, gain):
    wide = rows.astype(jnp.float32)
    squares = jnp.mean(wide * wide, axis=1, keepdims=True)
    return (wide * lax.rsqrt(squares + 1e-06) * gain).astype(jnp.bfloat16)


def values(rows, weight, head):
    hidden = jnp.dot(rows, weight, preferred_element_type=jnp.float32)
    half = 0.5 * hidden
    return jnp.sum((half + half * jnp.tanh(half)) * head, axis=1, keepdims=True)


def fetch_blocks(weights, blocks_ref, arrived):
    jobs = []
    for n, w_hbm in enumerate(weights):
        for start in range(0, w_hbm.shape[1], STEP):
            i = len(jobs)
            copy = pltpu.make_async_copy(w_hbm.at[:, pl.ds(start, STEP)], blocks_ref.at[i], arrived.at[i])
            copy.start()
            jobs.append((copy, n, start))
    return jobs


def score_own(x_ref, gain_ref, w_ref, h_ref, scaled_ref, value_ref):
    rows = scaled_rows(x_ref[...], gain_ref[...])
    scaled_ref[...] = rows
    value_ref[...] = values(rows, w_ref[...], h_ref[...].astype(jnp.float32))


def score_first(x_hbm, gain_ref, w_hbm, h_ref, scaled_ref, value_ref, x_ref, blocks_ref, rows_here, arrived):
    agents, slots, _ = x_ref.shape
    visit_copy = pltpu.make_async_copy(x_hbm, x_ref, rows_here.at[0])
    visit_copy.start()
    jobs = fetch_blocks((w_hbm,), blocks_ref, arrived)
    gain = gain_ref[...]
    head = h_ref[...].astype(jnp.float32)[0:1]
    visit_copy.wait()
    for start in range(0, agents, SCALE_AGENTS):
        rows = x_ref[start : start + SCALE_AGENTS].reshape(SCALE_AGENTS * slots, gain.shape[1])
        scaled_ref[start * slots : (start + SCALE_AGENTS) * slots, :] = scaled_rows(rows, gain)
    total = jnp.zeros(value_ref.shape, jnp.float32)
    for i, (copy, _, start) in enumerate(jobs):
        copy.wait()
        total += values(scaled_ref[...], blocks_ref[i], head[:, start : start + STEP])
    value_ref[...] = total


def score_last(
    visit_ref, visit_near_ref, own_ref, own_near_ref, w0_ref, h0_ref, w1_hbm, h1_ref, w2_hbm, w3_hbm, h23_ref,
    answer_out, value_out, total_ref, blocks_ref, arrived,
):
    jobs = fetch_blocks((w2_hbm, w1_hbm, w3_hbm), blocks_ref, arrived)
    far_heads = h23_ref[...].astype(jnp.float32)
    heads = (far_heads[0:1], h1_ref[...].astype(jnp.float32), far_heads[1:2])
    visit = visit_near_ref[...] + values(visit_ref[...], w0_ref[...], h0_ref[...].astype(jnp.float32))
    own = own_near_ref[...]
    for i, (copy, n, start) in enumerate(jobs):
        copy.wait()
        head = heads[n][:, start : start + STEP]
        own += values(own_ref[...], blocks_ref[i], head)
        if n > 0:
            visit += values(visit_ref[...], blocks_ref[i], head)
    total_ref[...] = visit
    agents, slots = answer_out.shape
    for k in range(slots):
        answer_out[:, k : k + 1] = total_ref[pl.ds(k, agents, stride=slots), :]
    owns = value_out.shape[1]
    value_out[...] = jnp.broadcast_to(own, (owns, owns)).T[0:1]


def score_call(body, operands, outs, weight, hbm=(), scratch=(), limit=0):
    vmem, anywhere = pl.BlockSpec(memory_space=pltpu.VMEM), pl.BlockSpec(memory_space=pl.ANY)
    return pl.pallas_call(
        body,
        in_specs=[anywhere if i in hbm else vmem for i in range(len(operands))],
        out_shape=outs,
        scratch_shapes=scratch,
        compiler_params=pltpu.CompilerParams(vmem_limit_bytes=limit or SCORE_VMEM),
        cost_estimate=hint(weight),
        name=body.__name__,
    )(*operands)


def per_device(observations, weights, gains, heads, pairing, valid):
    rows_dev, width = observations.shape
    n_agents = NZ * NXH * NY
    groups = exchange_groups()
    own_w = weights[0]
    exchange = ("z", "xh", "y", "xl")

    far_w = lax.ppermute(own_w, "xl", SWAP)
    owner = pairing.reshape(1, rows_dev)
    outgoing, slot = slots_call(owner, valid.reshape(1, rows_dev), observations, n_agents)
    near_h, slot = lax.optimization_barrier((heads, slot))
    received = lax.all_to_all(outgoing, exchange, 0, 0, axis_index_groups=groups, tiled=True)
    sib_h = lax.ppermute(near_h, "c", SWAP)
    near_w, sib_h = lax.optimization_barrier((own_w, sib_h))
    sib_w = lax.ppermute(near_w, "c", SWAP)
    far_h = lax.ppermute(jnp.concatenate([heads, sib_h], axis=0), "xl", SWAP)
    f32, bf16 = jnp.float32, jnp.bfloat16
    visits, units = 2 * n_agents, own_w.shape[1]
    shape = jax.ShapeDtypeStruct
    own_scaled, own_near = score_call(
        score_own,
        (observations, gains, own_w, heads),
        [pltpu.HBM((rows_dev, width), bf16), shape((rows_dev, 1), f32)],
        0,
    )
    far_w, far_h, own_scaled = lax.optimization_barrier((far_w, far_h, own_scaled))
    far_sib_w = lax.ppermute(far_w, "c", SWAP)
    blocks = units // STEP
    scaled, near = score_call(
        score_first,
        (received, gains, far_w, far_h),
        [shape((visits, width), bf16), shape((visits, 1), f32)],
        COST_FIRST,
        hbm=(0, 2),
        scratch=[
            pltpu.VMEM(received.shape, bf16),
            pltpu.VMEM((blocks, width, STEP), bf16),
            pltpu.SemaphoreType.DMA((1,)),
            pltpu.SemaphoreType.DMA((blocks,)),
        ],
        limit=REST_VMEM,
    )
    answers, own_value = score_call(
        score_last,
        (scaled, near, own_scaled, own_near, own_w, heads, sib_w, sib_h, far_w, far_sib_w, far_h),
        [shape((n_agents, 2), f32), shape((1, rows_dev), f32)],
        0,
        hbm=(6, 8, 9),
        scratch=[
            pltpu.VMEM((visits, 1), f32),
            pltpu.VMEM((3 * blocks, width, STEP), bf16),
            pltpu.SemaphoreType.DMA((3 * blocks,)),
        ],
        limit=REST_VMEM,
    )
    returned = lax.all_to_all(answers, exchange, 0, 0, axis_index_groups=groups, tiled=True)

    opponent_value = pick_call(returned, owner, slot)
    return own_value.reshape(rows_dev), opponent_value.reshape(rows_dev)


def solution(mesh):
    wide = Mesh(mesh.devices.reshape(NZ, NXH, NY, NXL, NC), AXES)
    league, rep = AXES[:3], AXES[3:]
    return jax.shard_map(
        per_device,
        mesh=wide,
        in_specs=(
            P(AXES, None),
            P(league, None, rep),
            P(league, None),
            P(league, rep),
            P(AXES, None),
            P(AXES),
        ),
        out_specs=(P(AXES), P(AXES)),
        check_vma=False,
    )
```

```python
import functools

import jax
import jax.numpy as jnp
from jax import lax
from jax.experimental import pallas as pl
from jax.experimental.pallas import tpu as pltpu
from jax.sharding import Mesh, PartitionSpec as P

NZ, NXH, NY, NXL, NC = 8, 2, 8, 2, 2
AXES = ("z", "xh", "y", "xl", "c")
SWAP = [(0, 1), (1, 0)]
COST_FIRST = 5
COST_OWN = 5
SLOTS_VMEM = 60 * 1024 * 1024
SCORE_VMEM = 16 * 1024 * 1024
REST_VMEM = 32 * 1024 * 1024
STEP = 512
SCALE_AGENTS = 32


def exchange_groups():
    groups = []
    for flip in range(2):
        group = []
        for z in range(NZ):
            for xh in range(NXH):
                for y in range(NY):
                    group.append(((z * NXH + xh) * NY + y) * NXL + (xh ^ flip))
        groups.append(group)
    return groups


def hint(weight):
    return pl.CostEstimate(flops=weight * 1_000_000_000, bytes_accessed=0, transcendentals=0)


def fill_slots(owner_hbm, valid_hbm, rows_hbm, out_ref, slot_ref, owner_ref, valid_ref, rows_ref, arrived):
    pairs = ((owner_hbm, owner_ref), (valid_hbm, valid_ref), (rows_hbm, rows_ref))
    copies = [pltpu.make_async_copy(src, dst, arrived.at[i]) for i, (src, dst) in enumerate(pairs)]
    for copy in copies:
        copy.start()
    count = owner_ref.shape[1]
    agents = out_ref.shape[0]
    copies[0].wait()
    copies[1].wait()
    owner = owner_ref[...]
    live = valid_ref[...]
    owner_down = jnp.broadcast_to(owner, (count, count)).T
    live_down = jnp.broadcast_to(live, (count, count)).T
    down = lax.broadcasted_iota(jnp.int32, (count, count), 0)
    across = lax.broadcasted_iota(jnp.int32, (count, count), 1)
    earlier = (owner_down == owner) & (live_down == 1) & (down < across)
    slot = jnp.sum(earlier.astype(jnp.int32), axis=0, keepdims=True)
    slot_ref[...] = jnp.where(live == 1, slot, 2)
    place = lax.broadcasted_iota(jnp.int32, (2 * agents, count), 0)
    pick = ((place == 2 * owner + slot) & (live == 1)).astype(jnp.float32).astype(jnp.bfloat16)
    copies[2].wait()
    out = jnp.dot(pick, rows_ref[...], preferred_element_type=jnp.float32).astype(jnp.bfloat16)
    out_ref[...] = out.reshape(out_ref.shape)


def slots_call(owner, valid, rows, agents):
    count, width = rows.shape
    return pl.pallas_call(
        fill_slots,
        in_specs=[pl.BlockSpec(memory_space=pltpu.HBM)] * 3,
        out_shape=[
            pltpu.HBM((agents, 2, width), jnp.bfloat16),
            jax.ShapeDtypeStruct((1, count), jnp.int32),
        ],
        scratch_shapes=[
            pltpu.VMEM(owner.shape, owner.dtype),
            pltpu.VMEM(valid.shape, valid.dtype),
            pltpu.VMEM(rows.shape, rows.dtype),
            pltpu.SemaphoreType.DMA((3,)),
        ],
        compiler_params=pltpu.CompilerParams(vmem_limit_bytes=SLOTS_VMEM),
        cost_estimate=hint(200),
        name="fill_slots",
    )(owner, valid, rows)


def pick_answers(returned_ref, owner_ref, slot_ref, out_ref):
    agents, count = returned_ref.shape[0], owner_ref.shape[1]
    slot = slot_ref[...]
    answer = jnp.where(slot == 0, returned_ref[:, 0:1], returned_ref[:, 1:2])
    agent = lax.broadcasted_iota(jnp.int32, (agents, count), 0)
    named = (agent == owner_ref[...]) & (slot < 2)
    out_ref[...] = jnp.sum(jnp.where(named, answer, 0.0), axis=0, keepdims=True)


def pick_call(returned, owner, slot):
    return pl.pallas_call(
        pick_answers,
        out_shape=jax.ShapeDtypeStruct(owner.shape, jnp.float32),
        compiler_params=pltpu.CompilerParams(vmem_limit_bytes=SCORE_VMEM),
        cost_estimate=hint(0),
        name="pick_answers",
    )(returned, owner, slot)


def scaled_rows(rows, gain):
    wide = rows.astype(jnp.float32)
    squares = jnp.mean(wide * wide, axis=1, keepdims=True)
    return (wide * lax.rsqrt(squares + 1e-06) * gain).astype(jnp.bfloat16)


def values(rows, weight, head):
    hidden = jnp.dot(rows, weight, preferred_element_type=jnp.float32)
    half = 0.5 * hidden
    return jnp.sum((half + half * jnp.tanh(half)) * head, axis=1, keepdims=True)


def fetch_blocks(weights, blocks_ref, arrived):
    jobs = []
    for n, w_hbm in enumerate(weights):
        for start in range(0, w_hbm.shape[1], STEP):
            i = len(jobs)
            copy = pltpu.make_async_copy(w_hbm.at[:, pl.ds(start, STEP)], blocks_ref.at[i], arrived.at[i])
            copy.start()
            jobs.append((copy, n, start))
    return jobs


def add_blocks(total, rows_ref, jobs, blocks_ref, heads):
    for i, (copy, n, start) in enumerate(jobs):
        copy.wait()
        total += values(rows_ref[...], blocks_ref[i], heads[n][:, start : start + STEP])
    return total


def score_own(x_ref, gain_ref, w_ref, h_ref, scaled_ref, value_ref):
    rows = scaled_rows(x_ref[...], gain_ref[...])
    scaled_ref[...] = rows
    value_ref[...] = values(rows, w_ref[...], h_ref[...].astype(jnp.float32))


def score_first(
    x_hbm, gain_ref, w0_ref, h0_ref, w1_hbm, h1_ref, scaled_ref, value_ref, x_ref, blocks_ref, rows_here, arrived
):
    agents, slots, _ = x_ref.shape
    visit_copy = pltpu.make_async_copy(x_hbm, x_ref, rows_here.at[0])
    visit_copy.start()
    jobs = fetch_blocks((w1_hbm,), blocks_ref, arrived)
    gain = gain_ref[...]
    visit_copy.wait()
    for start in range(0, agents, SCALE_AGENTS):
        rows = x_ref[start : start + SCALE_AGENTS].reshape(SCALE_AGENTS * slots, gain.shape[1])
        scaled_ref[start * slots : (start + SCALE_AGENTS) * slots, :] = scaled_rows(rows, gain)
    total = values(scaled_ref[...], w0_ref[...], h0_ref[...].astype(jnp.float32))
    value_ref[...] = add_blocks(total, scaled_ref, jobs, blocks_ref, (h1_ref[...].astype(jnp.float32)[0:1],))


def score_last(scaled_ref, near_ref, w0_hbm, h0_ref, w1_hbm, h1_ref, answer_out, total_ref, blocks_ref, arrived):
    jobs = fetch_blocks((w0_hbm, w1_hbm), blocks_ref, arrived)
    heads = (h0_ref[...].astype(jnp.float32), h1_ref[...].astype(jnp.float32)[1:2])
    total_ref[...] = add_blocks(near_ref[...], scaled_ref, jobs, blocks_ref, heads)
    agents, slots = answer_out.shape
    for k in range(slots):
        answer_out[:, k : k + 1] = total_ref[pl.ds(k, agents, stride=slots), :]


def score_own_rest(scaled_ref, near_ref, w0_hbm, h0_ref, w1_hbm, w2_hbm, h12_ref, value_out, blocks_ref, arrived):
    jobs = fetch_blocks((w0_hbm, w1_hbm, w2_hbm), blocks_ref, arrived)
    far_heads = h12_ref[...].astype(jnp.float32)
    heads = (h0_ref[...].astype(jnp.float32), far_heads[0:1], far_heads[1:2])
    total = add_blocks(near_ref[...], scaled_ref, jobs, blocks_ref, heads)
    owns = value_out.shape[1]
    value_out[...] = jnp.broadcast_to(total, (owns, owns)).T[0:1]


def score_call(body, operands, outs, weight, hbm=(), scratch=(), limit=0):
    vmem, anywhere = pl.BlockSpec(memory_space=pltpu.VMEM), pl.BlockSpec(memory_space=pl.ANY)
    return pl.pallas_call(
        body,
        in_specs=[anywhere if i in hbm else vmem for i in range(len(operands))],
        out_shape=outs,
        scratch_shapes=scratch,
        compiler_params=pltpu.CompilerParams(vmem_limit_bytes=limit or SCORE_VMEM),
        cost_estimate=hint(weight),
        name=body.__name__,
    )(*operands)


def per_device(observations, weights, gains, heads, pairing, valid):
    rows_dev, width = observations.shape
    n_agents = NZ * NXH * NY
    groups = exchange_groups()
    own_w = weights[0]
    exchange = ("z", "xh", "y", "xl")

    far_w = lax.ppermute(own_w, "xl", SWAP)
    owner = pairing.reshape(1, rows_dev)
    outgoing, slot = slots_call(owner, valid.reshape(1, rows_dev), observations, n_agents)
    near_h, slot = lax.optimization_barrier((heads, slot))
    received = lax.all_to_all(outgoing, exchange, 0, 0, axis_index_groups=groups, tiled=True)
    sib_h = lax.ppermute(near_h, "c", SWAP)
    near_w, sib_h = lax.optimization_barrier((own_w, sib_h))
    sib_w = lax.ppermute(near_w, "c", SWAP)
    far_h = lax.ppermute(jnp.concatenate([heads, sib_h], axis=0), "xl", SWAP)
    f32, bf16 = jnp.float32, jnp.bfloat16
    visits, units = 2 * n_agents, own_w.shape[1]
    shape = jax.ShapeDtypeStruct
    own_scaled, own_near = score_call(
        score_own,
        (observations, gains, own_w, heads),
        [pltpu.HBM((rows_dev, width), bf16), shape((rows_dev, 1), f32)],
        0,
    )
    far_w, far_h, own_scaled = lax.optimization_barrier((far_w, far_h, own_scaled))
    far_sib_w = lax.ppermute(far_w, "c", SWAP)
    blocks = units // STEP

    def copied(count):
        return [pltpu.VMEM((count * blocks, width, STEP), bf16), pltpu.SemaphoreType.DMA((count * blocks,))]

    fetched, here = copied(1)
    scaled, near = score_call(
        score_first,
        (received, gains, own_w, heads, far_w, far_h),
        [shape((visits, width), bf16), shape((visits, 1), f32)],
        COST_FIRST,
        hbm=(0, 4),
        scratch=[pltpu.VMEM(received.shape, bf16), fetched, pltpu.SemaphoreType.DMA((1,)), here],
        limit=REST_VMEM,
    )
    answers = score_call(
        score_last,
        (scaled, near, sib_w, sib_h, far_sib_w, far_h),
        shape((n_agents, 2), f32),
        0,
        hbm=(2, 4),
        scratch=[pltpu.VMEM((visits, 1), f32)] + copied(2),
        limit=REST_VMEM,
    )
    returned = lax.all_to_all(answers, exchange, 0, 0, axis_index_groups=groups, tiled=True)
    own_scaled, answers = lax.optimization_barrier((own_scaled, answers))
    own_value = score_call(
        score_own_rest,
        (own_scaled, own_near, sib_w, sib_h, far_w, far_sib_w, far_h),
        shape((1, rows_dev), f32),
        COST_OWN,
        hbm=(2, 4, 5),
        scratch=copied(3),
        limit=REST_VMEM,
    )
    opponent_value = pick_call(returned, owner, slot)
    return own_value.reshape(rows_dev), opponent_value.reshape(rows_dev)


def solution(mesh):
    wide = Mesh(mesh.devices.reshape(NZ, NXH, NY, NXL, NC), AXES)
    league, rep = AXES[:3], AXES[3:]
    return jax.shard_map(
        per_device,
        mesh=wide,
        in_specs=(
            P(AXES, None),
            P(league, None, rep),
            P(league, None),
            P(league, rep),
            P(AXES, None),
            P(AXES),
        ),
        out_specs=(P(AXES), P(AXES)),
        check_vma=False,
    )
```

```python
import functools

import jax
import jax.numpy as jnp
from jax import lax
from jax.experimental import pallas as pl
from jax.experimental.pallas import tpu as pltpu
from jax.sharding import Mesh, PartitionSpec as P

NZ, NXH, NY, NXL, NC = 8, 2, 8, 2, 2
AXES = ("z", "xh", "y", "xl", "c")
SWAP = [(0, 1), (1, 0)]
COST_FIRST = 5
COST_OWN = 5
SLOTS_VMEM = 60 * 1024 * 1024
SCORE_VMEM = 16 * 1024 * 1024
REST_VMEM = 32 * 1024 * 1024
STEP = 512
SCALE_AGENTS = 32


def exchange_groups():
    groups = []
    for flip in range(2):
        group = []
        for z in range(NZ):
            for xh in range(NXH):
                for y in range(NY):
                    group.append(((z * NXH + xh) * NY + y) * NXL + (xh ^ flip))
        groups.append(group)
    return groups


def hint(weight):
    return pl.CostEstimate(flops=weight * 1_000_000_000, bytes_accessed=0, transcendentals=0)


def fill_slots(owner_hbm, valid_hbm, rows_hbm, out_ref, slot_ref, owner_ref, valid_ref, rows_ref, arrived):
    pairs = ((owner_hbm, owner_ref), (valid_hbm, valid_ref), (rows_hbm, rows_ref))
    copies = [pltpu.make_async_copy(src, dst, arrived.at[i]) for i, (src, dst) in enumerate(pairs)]
    for copy in copies:
        copy.start()
    count = owner_ref.shape[1]
    agents = out_ref.shape[0]
    copies[0].wait()
    copies[1].wait()
    owner = owner_ref[...]
    live = valid_ref[...]
    owner_down = jnp.broadcast_to(owner, (count, count)).T
    live_down = jnp.broadcast_to(live, (count, count)).T
    down = lax.broadcasted_iota(jnp.int32, (count, count), 0)
    across = lax.broadcasted_iota(jnp.int32, (count, count), 1)
    earlier = (owner_down == owner) & (live_down == 1) & (down < across)
    slot = jnp.sum(earlier.astype(jnp.int32), axis=0, keepdims=True)
    slot_ref[...] = jnp.where(live == 1, slot, 2)
    place = lax.broadcasted_iota(jnp.int32, (2 * agents, count), 0)
    pick = ((place == 2 * owner + slot) & (live == 1)).astype(jnp.float32).astype(jnp.bfloat16)
    copies[2].wait()
    out = jnp.dot(pick, rows_ref[...], preferred_element_type=jnp.float32).astype(jnp.bfloat16)
    out_ref[...] = out.reshape(out_ref.shape)


def slots_call(owner, valid, rows, agents):
    count, width = rows.shape
    return pl.pallas_call(
        fill_slots,
        in_specs=[pl.BlockSpec(memory_space=pltpu.HBM)] * 3,
        out_shape=[
            pltpu.HBM((agents, 2, width), jnp.bfloat16),
            jax.ShapeDtypeStruct((1, count), jnp.int32),
        ],
        scratch_shapes=[
            pltpu.VMEM(owner.shape, owner.dtype),
            pltpu.VMEM(valid.shape, valid.dtype),
            pltpu.VMEM(rows.shape, rows.dtype),
            pltpu.SemaphoreType.DMA((3,)),
        ],
        compiler_params=pltpu.CompilerParams(vmem_limit_bytes=SLOTS_VMEM),
        cost_estimate=hint(200),
        name="fill_slots",
    )(owner, valid, rows)


def pick_answers(returned_ref, owner_ref, slot_ref, out_ref):
    agents, count = returned_ref.shape[0], owner_ref.shape[1]
    slot = slot_ref[...]
    answer = jnp.where(slot == 0, returned_ref[:, 0:1], returned_ref[:, 1:2])
    agent = lax.broadcasted_iota(jnp.int32, (agents, count), 0)
    named = (agent == owner_ref[...]) & (slot < 2)
    out_ref[...] = jnp.sum(jnp.where(named, answer, 0.0), axis=0, keepdims=True)


def pick_call(returned, owner, slot):
    return pl.pallas_call(
        pick_answers,
        out_shape=jax.ShapeDtypeStruct(owner.shape, jnp.float32),
        compiler_params=pltpu.CompilerParams(vmem_limit_bytes=SCORE_VMEM),
        cost_estimate=hint(0),
        name="pick_answers",
    )(returned, owner, slot)


def scaled_rows(rows, gain):
    wide = rows.astype(jnp.float32)
    squares = jnp.mean(wide * wide, axis=1, keepdims=True)
    return (wide * lax.rsqrt(squares + 1e-06) * gain).astype(jnp.bfloat16)


def values(rows, weight, head):
    hidden = jnp.dot(rows, weight, preferred_element_type=jnp.float32)
    half = 0.5 * hidden
    return jnp.sum((half + half * jnp.tanh(half)) * head, axis=1, keepdims=True)


def fetch_blocks(weights, blocks_ref, arrived):
    jobs = []
    for n, w_hbm in enumerate(weights):
        for start in range(0, w_hbm.shape[1], STEP):
            i = len(jobs)
            copy = pltpu.make_async_copy(w_hbm.at[:, pl.ds(start, STEP)], blocks_ref.at[i], arrived.at[i])
            copy.start()
            jobs.append((copy, n, start))
    return jobs


def add_blocks(total, rows_ref, jobs, blocks_ref, heads):
    for i, (copy, n, start) in enumerate(jobs):
        copy.wait()
        total += values(rows_ref[...], blocks_ref[i], heads[n][:, start : start + STEP])
    return total


def score_own(x_ref, gain_ref, w_ref, h_ref, scaled_ref, value_ref):
    rows = scaled_rows(x_ref[...], gain_ref[...])
    scaled_ref[...] = rows
    value_ref[...] = values(rows, w_ref[...], h_ref[...].astype(jnp.float32))


def score_first(
    x_hbm, gain_ref, w0_ref, h0_ref, w1_hbm, h1_ref, scaled_ref, value_ref, x_ref, blocks_ref, rows_here, arrived
):
    agents, slots, _ = x_ref.shape
    visit_copy = pltpu.make_async_copy(x_hbm, x_ref, rows_here.at[0])
    visit_copy.start()
    jobs = fetch_blocks((w1_hbm,), blocks_ref, arrived)
    gain = gain_ref[...]
    visit_copy.wait()
    for start in range(0, agents, SCALE_AGENTS):
        rows = x_ref[start : start + SCALE_AGENTS].reshape(SCALE_AGENTS * slots, gain.shape[1])
        scaled_ref[start * slots : (start + SCALE_AGENTS) * slots, :] = scaled_rows(rows, gain)
    total = values(scaled_ref[...], w0_ref[...], h0_ref[...].astype(jnp.float32))
    value_ref[...] = add_blocks(total, scaled_ref, jobs, blocks_ref, (h1_ref[...].astype(jnp.float32)[0:1],))


def score_middle(scaled_ref, near_ref, w_hbm, h_ref, value_ref, blocks_ref, arrived):
    jobs = fetch_blocks((w_hbm,), blocks_ref, arrived)
    value_ref[...] = add_blocks(near_ref[...], scaled_ref, jobs, blocks_ref, (h_ref[...].astype(jnp.float32),))


def score_last(scaled_ref, near_ref, w_hbm, h_ref, answer_out, total_ref, blocks_ref, arrived):
    jobs = fetch_blocks((w_hbm,), blocks_ref, arrived)
    head = h_ref[...].astype(jnp.float32)[1:2]
    total_ref[...] = add_blocks(near_ref[...], scaled_ref, jobs, blocks_ref, (head,))
    agents, slots = answer_out.shape
    for k in range(slots):
        answer_out[:, k : k + 1] = total_ref[pl.ds(k, agents, stride=slots), :]


def score_own_rest(scaled_ref, near_ref, w0_hbm, h0_ref, w1_hbm, w2_hbm, h12_ref, value_out, blocks_ref, arrived):
    jobs = fetch_blocks((w0_hbm, w1_hbm, w2_hbm), blocks_ref, arrived)
    far_heads = h12_ref[...].astype(jnp.float32)
    heads = (h0_ref[...].astype(jnp.float32), far_heads[0:1], far_heads[1:2])
    total = add_blocks(near_ref[...], scaled_ref, jobs, blocks_ref, heads)
    owns = value_out.shape[1]
    value_out[...] = jnp.broadcast_to(total, (owns, owns)).T[0:1]


def score_call(body, operands, outs, weight, hbm=(), scratch=(), limit=0):
    vmem, anywhere = pl.BlockSpec(memory_space=pltpu.VMEM), pl.BlockSpec(memory_space=pl.ANY)
    return pl.pallas_call(
        body,
        in_specs=[anywhere if i in hbm else vmem for i in range(len(operands))],
        out_shape=outs,
        scratch_shapes=scratch,
        compiler_params=pltpu.CompilerParams(vmem_limit_bytes=limit or SCORE_VMEM),
        cost_estimate=hint(weight),
        name=body.__name__,
    )(*operands)


def per_device(observations, weights, gains, heads, pairing, valid):
    rows_dev, width = observations.shape
    n_agents = NZ * NXH * NY
    groups = exchange_groups()
    own_w = weights[0]
    exchange = ("z", "xh", "y", "xl")

    far_w = lax.ppermute(own_w, "xl", SWAP)
    owner = pairing.reshape(1, rows_dev)
    outgoing, slot = slots_call(owner, valid.reshape(1, rows_dev), observations, n_agents)
    near_h, slot = lax.optimization_barrier((heads, slot))
    received = lax.all_to_all(outgoing, exchange, 0, 0, axis_index_groups=groups, tiled=True)
    sib_h = lax.ppermute(near_h, "c", SWAP)
    near_w, sib_h = lax.optimization_barrier((own_w, sib_h))
    sib_w = lax.ppermute(near_w, "c", SWAP)
    far_h = lax.ppermute(jnp.concatenate([heads, sib_h], axis=0), "xl", SWAP)
    f32, bf16 = jnp.float32, jnp.bfloat16
    visits, units = 2 * n_agents, own_w.shape[1]
    shape = jax.ShapeDtypeStruct
    own_scaled, own_near = score_call(
        score_own,
        (observations, gains, own_w, heads),
        [pltpu.HBM((rows_dev, width), bf16), shape((rows_dev, 1), f32)],
        0,
    )
    far_w, far_h, own_scaled = lax.optimization_barrier((far_w, far_h, own_scaled))
    far_sib_w = lax.ppermute(far_w, "c", SWAP)
    blocks = units // STEP

    def copied(count):
        return [pltpu.VMEM((count * blocks, width, STEP), bf16), pltpu.SemaphoreType.DMA((count * blocks,))]

    fetched, here = copied(1)
    scaled, near = score_call(
        score_first,
        (received, gains, own_w, heads, far_w, far_h),
        [shape((visits, width), bf16), shape((visits, 1), f32)],
        COST_FIRST,
        hbm=(0, 4),
        scratch=[pltpu.VMEM(received.shape, bf16), fetched, pltpu.SemaphoreType.DMA((1,)), here],
        limit=REST_VMEM,
    )
    near = score_call(
        score_middle, (scaled, near, sib_w, sib_h), shape((visits, 1), f32), 0, hbm=(2,), scratch=copied(1), limit=REST_VMEM
    )
    answers = score_call(
        score_last,
        (scaled, near, far_sib_w, far_h),
        shape((n_agents, 2), f32),
        0,
        hbm=(2,),
        scratch=[pltpu.VMEM((visits, 1), f32)] + copied(1),
        limit=REST_VMEM,
    )
    returned = lax.all_to_all(answers, exchange, 0, 0, axis_index_groups=groups, tiled=True)
    own_scaled, answers = lax.optimization_barrier((own_scaled, answers))
    own_value = score_call(
        score_own_rest,
        (own_scaled, own_near, sib_w, sib_h, far_w, far_sib_w, far_h),
        shape((1, rows_dev), f32),
        COST_OWN,
        hbm=(2, 4, 5),
        scratch=copied(3),
        limit=REST_VMEM,
    )
    opponent_value = pick_call(returned, owner, slot)
    return own_value.reshape(rows_dev), opponent_value.reshape(rows_dev)


def solution(mesh):
    wide = Mesh(mesh.devices.reshape(NZ, NXH, NY, NXL, NC), AXES)
    league, rep = AXES[:3], AXES[3:]
    return jax.shard_map(
        per_device,
        mesh=wide,
        in_specs=(
            P(AXES, None),
            P(league, None, rep),
            P(league, None),
            P(league, rep),
            P(AXES, None),
            P(AXES),
        ),
        out_specs=(P(AXES), P(AXES)),
        check_vma=False,
    )
```

```python
import functools

import jax
import jax.numpy as jnp
from jax import lax
from jax.experimental import pallas as pl
from jax.experimental.pallas import tpu as pltpu
from jax.sharding import Mesh, PartitionSpec as P

NZ, NXH, NY, NXL, NC = 8, 2, 8, 2, 2
AXES = ("z", "xh", "y", "xl", "c")
SWAP = [(0, 1), (1, 0)]
COST_FIRST = 20
COST_OWN = 5
SLOTS_VMEM = 60 * 1024 * 1024
SCORE_VMEM = 16 * 1024 * 1024
REST_VMEM = 32 * 1024 * 1024
SCALE_AGENTS = 32


def exchange_groups():
    groups = []
    for flip in range(2):
        group = []
        for z in range(NZ):
            for xh in range(NXH):
                for y in range(NY):
                    group.append(((z * NXH + xh) * NY + y) * NXL + (xh ^ flip))
        groups.append(group)
    return groups


def hint(weight):
    return pl.CostEstimate(flops=weight * 1_000_000_000, bytes_accessed=0, transcendentals=0)


def fill_slots(owner_hbm, valid_hbm, rows_hbm, out_ref, slot_ref, owner_ref, valid_ref, rows_ref, arrived):
    pairs = ((owner_hbm, owner_ref), (valid_hbm, valid_ref), (rows_hbm, rows_ref))
    copies = [pltpu.make_async_copy(src, dst, arrived.at[i]) for i, (src, dst) in enumerate(pairs)]
    for copy in copies:
        copy.start()
    count = owner_ref.shape[1]
    agents = out_ref.shape[0]
    copies[0].wait()
    copies[1].wait()
    owner = owner_ref[...]
    live = valid_ref[...]
    owner_down = jnp.broadcast_to(owner, (count, count)).T
    live_down = jnp.broadcast_to(live, (count, count)).T
    down = lax.broadcasted_iota(jnp.int32, (count, count), 0)
    across = lax.broadcasted_iota(jnp.int32, (count, count), 1)
    earlier = (owner_down == owner) & (live_down == 1) & (down < across)
    slot = jnp.sum(earlier.astype(jnp.int32), axis=0, keepdims=True)
    slot_ref[...] = jnp.where(live == 1, slot, 2)
    place = lax.broadcasted_iota(jnp.int32, (2 * agents, count), 0)
    pick = ((place == 2 * owner + slot) & (live == 1)).astype(jnp.float32).astype(jnp.bfloat16)
    copies[2].wait()
    out = jnp.dot(pick, rows_ref[...], preferred_element_type=jnp.float32).astype(jnp.bfloat16)
    out_ref[...] = out.reshape(out_ref.shape)


def slots_call(owner, valid, rows, agents):
    count, width = rows.shape
    return pl.pallas_call(
        fill_slots,
        in_specs=[pl.BlockSpec(memory_space=pltpu.HBM)] * 3,
        out_shape=[
            pltpu.HBM((agents, 2, width), jnp.bfloat16),
            jax.ShapeDtypeStruct((1, count), jnp.int32),
        ],
        scratch_shapes=[
            pltpu.VMEM(owner.shape, owner.dtype),
            pltpu.VMEM(valid.shape, valid.dtype),
            pltpu.VMEM(rows.shape, rows.dtype),
            pltpu.SemaphoreType.DMA((3,)),
        ],
        compiler_params=pltpu.CompilerParams(vmem_limit_bytes=SLOTS_VMEM),
        cost_estimate=hint(200),
        name="fill_slots",
    )(owner, valid, rows)


def pick_answers(returned_ref, owner_ref, slot_ref, out_ref):
    agents, count = returned_ref.shape[0], owner_ref.shape[1]
    slot = slot_ref[...]
    answer = jnp.where(slot == 0, returned_ref[:, 0:1], returned_ref[:, 1:2])
    agent = lax.broadcasted_iota(jnp.int32, (agents, count), 0)
    named = (agent == owner_ref[...]) & (slot < 2)
    out_ref[...] = jnp.sum(jnp.where(named, answer, 0.0), axis=0, keepdims=True)


def pick_call(returned, owner, slot):
    return pl.pallas_call(
        pick_answers,
        out_shape=jax.ShapeDtypeStruct(owner.shape, jnp.float32),
        compiler_params=pltpu.CompilerParams(vmem_limit_bytes=SCORE_VMEM),
        cost_estimate=hint(0),
        name="pick_answers",
    )(returned, owner, slot)


def scaled_rows(rows, gain):
    wide = rows.astype(jnp.float32)
    squares = jnp.mean(wide * wide, axis=1, keepdims=True)
    return (wide * lax.rsqrt(squares + 1e-06) * gain).astype(jnp.bfloat16)


def values(rows, weight, head):
    hidden = jnp.dot(rows, weight, preferred_element_type=jnp.float32)
    half = 0.5 * hidden
    return jnp.sum((half + half * jnp.tanh(half)) * head, axis=1, keepdims=True)


def fetch_blocks(weights, blocks_ref, arrived):
    jobs, started = [], 0
    for i, parts in enumerate(weights):
        copies, top = [], 0
        for part in parts:
            rows = part.shape[0]
            copy = pltpu.make_async_copy(part, blocks_ref.at[i, pl.ds(top, rows), :], arrived.at[started])
            copy.start()
            copies.append(copy)
            started, top = started + 1, top + rows
        jobs.append(copies)
    return jobs


def add_blocks(total, rows_ref, jobs, blocks_ref, heads):
    for i, copies in enumerate(jobs):
        for copy in copies:
            copy.wait()
        total += values(rows_ref[...], blocks_ref[i], heads[i])
    return total


def score_own(x_ref, gain_ref, w_ref, h_ref, scaled_ref, value_ref):
    rows = scaled_rows(x_ref[...], gain_ref[...])
    scaled_ref[...] = rows
    value_ref[...] = values(rows, w_ref[...], h_ref[...].astype(jnp.float32))


def score_first(
    x_ref, gain_ref, w0_ref, h0_ref, w1a_hbm, w1b_hbm, h1_ref, scaled_ref, value_ref, blocks_ref, arrived
):
    agents, slots, _ = x_ref.shape
    jobs = fetch_blocks(((w1a_hbm, w1b_hbm),), blocks_ref, arrived)
    gain = gain_ref[...]
    for start in range(0, agents, SCALE_AGENTS):
        rows = x_ref[start : start + SCALE_AGENTS].reshape(SCALE_AGENTS * slots, gain.shape[1])
        scaled_ref[start * slots : (start + SCALE_AGENTS) * slots, :] = scaled_rows(rows, gain)
    total = values(scaled_ref[...], w0_ref[...], h0_ref[...].astype(jnp.float32))
    value_ref[...] = add_blocks(total, scaled_ref, jobs, blocks_ref, (h1_ref[...].astype(jnp.float32)[0:1],))


def score_last(scaled_ref, near_ref, w0_hbm, h0_ref, w1a_hbm, w1b_hbm, h1_ref, answer_out, total_ref, blocks_ref, arrived):
    jobs = fetch_blocks(((w0_hbm,), (w1a_hbm, w1b_hbm)), blocks_ref, arrived)
    heads = (h0_ref[...].astype(jnp.float32), h1_ref[...].astype(jnp.float32)[1:2])
    total_ref[...] = add_blocks(near_ref[...], scaled_ref, jobs, blocks_ref, heads)
    agents, slots = answer_out.shape
    for k in range(slots):
        answer_out[:, k : k + 1] = total_ref[pl.ds(k, agents, stride=slots), :]


def score_own_rest(
    scaled_ref, near_ref, w0_hbm, h0_ref, w1a_hbm, w1b_hbm, w2a_hbm, w2b_hbm, h12_ref, value_out, blocks_ref, arrived
):
    jobs = fetch_blocks(((w0_hbm,), (w1a_hbm, w1b_hbm), (w2a_hbm, w2b_hbm)), blocks_ref, arrived)
    far_heads = h12_ref[...].astype(jnp.float32)
    heads = (h0_ref[...].astype(jnp.float32), far_heads[0:1], far_heads[1:2])
    total = add_blocks(near_ref[...], scaled_ref, jobs, blocks_ref, heads)
    owns = value_out.shape[1]
    value_out[...] = jnp.broadcast_to(total, (owns, owns)).T[0:1]


def score_call(body, operands, outs, weight, hbm=(), scratch=(), limit=0):
    vmem, anywhere = pl.BlockSpec(memory_space=pltpu.VMEM), pl.BlockSpec(memory_space=pl.ANY)
    return pl.pallas_call(
        body,
        in_specs=[anywhere if i in hbm else vmem for i in range(len(operands))],
        out_shape=outs,
        scratch_shapes=scratch,
        compiler_params=pltpu.CompilerParams(vmem_limit_bytes=limit or SCORE_VMEM),
        cost_estimate=hint(weight),
        name=body.__name__,
    )(*operands)


def per_device(observations, weights, gains, heads, pairing, valid):
    rows_dev, width = observations.shape
    n_agents = NZ * NXH * NY
    groups = exchange_groups()
    own_w = weights[0]
    exchange = ("z", "xh", "y", "xl")

    half = width // 2
    far_a = lax.ppermute(own_w[:half], "xl", SWAP)
    far_b = lax.ppermute(own_w[half:], "xl", SWAP)
    far_sib_a = lax.ppermute(far_a, "c", SWAP)
    owner = pairing.reshape(1, rows_dev)
    outgoing, slot = slots_call(owner, valid.reshape(1, rows_dev), observations, n_agents)
    near_h, slot = lax.optimization_barrier((heads, slot))
    received = lax.all_to_all(outgoing, exchange, 0, 0, axis_index_groups=groups, tiled=True)
    sib_h = lax.ppermute(near_h, "c", SWAP)
    near_w, sib_h = lax.optimization_barrier((own_w, sib_h))
    sib_w = lax.ppermute(near_w, "c", SWAP)
    far_h = lax.ppermute(jnp.concatenate([heads, sib_h], axis=0), "xl", SWAP)
    f32, bf16 = jnp.float32, jnp.bfloat16
    visits, units = 2 * n_agents, own_w.shape[1]
    shape = jax.ShapeDtypeStruct
    own_scaled, own_near = score_call(
        score_own,
        (observations, gains, own_w, heads),
        [pltpu.HBM((rows_dev, width), bf16), shape((rows_dev, 1), f32)],
        0,
    )
    far_b, far_sib_a, far_h, own_scaled = lax.optimization_barrier((far_b, far_sib_a, far_h, own_scaled))
    far_sib_b = lax.ppermute(far_b, "c", SWAP)

    def copied(count):
        return [pltpu.VMEM((count, width, units), bf16), pltpu.SemaphoreType.DMA((2 * count,))]

    scaled, near = score_call(
        score_first,
        (received, gains, own_w, heads, far_a, far_b, far_h),
        [shape((visits, width), bf16), shape((visits, 1), f32)],
        COST_FIRST,
        hbm=(4, 5),
        scratch=copied(1),
        limit=REST_VMEM,
    )
    answers = score_call(
        score_last,
        (scaled, near, sib_w, sib_h, far_sib_a, far_sib_b, far_h),
        shape((n_agents, 2), f32),
        0,
        hbm=(2, 4, 5),
        scratch=[pltpu.VMEM((visits, 1), f32)] + copied(2),
        limit=REST_VMEM,
    )
    returned = lax.all_to_all(answers, exchange, 0, 0, axis_index_groups=groups, tiled=True)
    own_scaled, answers = lax.optimization_barrier((own_scaled, answers))
    own_value = score_call(
        score_own_rest,
        (own_scaled, own_near, sib_w, sib_h, far_a, far_b, far_sib_a, far_sib_b, far_h),
        shape((1, rows_dev), f32),
        COST_OWN,
        hbm=(2, 4, 5, 6, 7),
        scratch=copied(3),
        limit=REST_VMEM,
    )
    opponent_value = pick_call(returned, owner, slot)
    return own_value.reshape(rows_dev), opponent_value.reshape(rows_dev)


def solution(mesh):
    wide = Mesh(mesh.devices.reshape(NZ, NXH, NY, NXL, NC), AXES)
    league, rep = AXES[:3], AXES[3:]
    return jax.shard_map(
        per_device,
        mesh=wide,
        in_specs=(
            P(AXES, None),
            P(league, None, rep),
            P(league, None),
            P(league, rep),
            P(AXES, None),
            P(AXES),
        ),
        out_specs=(P(AXES), P(AXES)),
        check_vma=False,
    )
```
